256 devices in a mesh: shock: 16 (over y, x_lo, core), trans: 16 (over z, x_hi).
Axes of the slice: x: 4 (x_hi: 2, x_lo: 2; x = x_hi * 2 + x_lo), y: 4, z: 8, core: 2. Of those that a mesh axis runs over, the one named last changes fastest.
Arguments:
- positions: float32 [32, 16, 3, 128], P('shock', 'trans'), may hold values from 0.35 to 12.8, as said below
- velocities: float32 [32, 16, 3, 128], P('shock', 'trans'), may hold values from -3 to 3
- features: bfloat16 [32, 16, 576, 128], P('shock', 'trans'), may hold values from -6 to 6
- neighbours: int32 [32, 16, 24, 128], P('shock', 'trans'), may hold values from 0 to 3455, as said below
- counts: int32 [32, 16, 128], P('shock', 'trans'), may hold values from 12 to 24, as said below
- w_first: float32 [64, 8], replicated, may hold values from -2 to 2
- w_second: float32 [192, 64], replicated, may hold values from -0.75 to 0.75
- w_read: float32 [128, 192], replicated, may hold values from -0.4375 to 0.4375
- w_out: float32 [128], replicated, may hold values from -0.5 to 0.5
- fresh_positions: float32 [16, 3, 128], P('trans'), may hold values from 0.35 to 12.8, as said below
- fresh_velocities: float32 [16, 3, 128], P('trans'), may hold values from -3 to 3
Outputs:
- energies: float32 [32, 16, 128], P('shock', 'trans')
- new_positions: float32 [32, 16, 3, 128], P('shock', 'trans')
- new_velocities: float32 [32, 16, 3, 128], P('shock', 'trans')
The draws below stay inside these ranges and needn't reach their ends.
Inputs may be any that keep to these rules, and one draw needn't show every extreme that they name: `positions`: Block-local coordinates of each block's 128 atoms lie near the sites of a body-centred cubic arrangement of 4 x 4 x 4 cells of side 3.3 inside a cube of side 13.2. `fresh_positions`: as for positions. `neighbours`: each code is ((dz + 1) * 9 + (ds + 1) * 3 + (dt + 1)) * 128 + j with ds, dt, dz in -1 .. 1, naming a lattice neighbour of the atom other than itself at a distance between 1.2 and 8.8; codes of an atom are distinct. `counts`: slots at or beyond an atom's count are padding. Every atom of the block rows below 16 has all 24 slots live.
All inputs are finite; a program needn't handle non-finite values.
Results may differ from the reference program's by a relative error of at most 0.0006.
Values may be sent and summed in bfloat16 or wider, within the bound.
A program may use at most 128 MiB of HBM per device.

```python
import math
import jax
import jax.numpy as jnp
import numpy as np
from jax import lax

CH = 64
COMP = 9
NB = 8
RH = 64
EH = 128
NBR = 24
NSB = 32
NTB = 16


def lattice_sites():
    atom_ids = jnp.arange(128, dtype=jnp.int32)
    basis_bit = atom_ids % 2
    cell_id = atom_ids // 2
    return jnp.stack([2 * (cell_id // 16) + basis_bit, 2 * (cell_id // 4 % 4) + basis_bit, 2 * (cell_id % 4) + basis_bit])


def jittered(key, leading):
    centre = lattice_sites().astype(jnp.float32) * 1.65 + 0.8
    shape = leading + (3, 128)
    jitter = jax.random.uniform(key, shape, jnp.float32, -0.45, 0.45)
    return centre + jitter


def draw_positions(key, part):
    return jittered(jax.random.fold_in(key, 3), (NSB, NTB))


def draw_fresh_positions(key, part):
    return jittered(jax.random.fold_in(key, 5), (NTB,))


def candidate_table():
    found = []
    for step_x in range(-4, 5):
        for step_y in range(-4, 5):
            for step_z in range(-4, 5):
                same = step_x % 2 == step_y % 2 and step_y % 2 == step_z % 2
                square = step_x * step_x + step_y * step_y + step_z * step_z
                if same and 0 < square <= 19:
                    found.append([step_x, step_y, step_z])
    return np.array(found, dtype=np.int32)


def draw_neighbours(key, part):
    table = jnp.asarray(candidate_table())
    total = table.shape[0]
    scores = jax.random.randint(jax.random.fold_in(key, 11), (NSB, NTB, 128, total), 0, 1 << 20) * 128
    scores = scores + jnp.arange(total, dtype=jnp.int32)
    chosen = jnp.argsort(scores, axis=-1, stable=True)[..., :NBR]
    moves = table[chosen]
    sites = lattice_sites().T[None, None, :, None, :]
    target = sites + moves
    block_shift = jnp.floor_divide(target, 8)
    local = target - 8 * block_shift
    parity = local[..., 0] % 2
    cells = (local - parity[..., None]) // 2
    atom_ids = ((cells[..., 0] * 4 + cells[..., 1]) * 4 + cells[..., 2]) * 2 + parity
    codes = ((block_shift[..., 2] + 1) * 9 + (block_shift[..., 0] + 1) * 3 + (block_shift[..., 1] + 1)) * 128 + atom_ids
    return jnp.moveaxis(codes, 3, 2).astype(jnp.int32)


def draw_counts(key, part):
    block_rows = lax.broadcasted_iota(jnp.int32, (NSB, NTB, 128), 0)
    spread = jax.random.randint(jax.random.fold_in(key, 13), (NSB, NTB, 128), NBR // 2, NBR * 3 // 4 + 1)
    return jnp.where(block_rows < NSB // 2, NBR, spread).astype(jnp.int32)


def level_of(rng, extent, cuts, low, largest):
    factor_of = 1.0
    for dim, blocks in cuts:
        steps = jax.random.uniform(jax.random.fold_in(jax.random.fold_in(rng, 6), dim), (blocks,), jnp.float32, low / len(cuts), largest / len(cuts))
        factor_of = factor_of * jnp.repeat(jnp.exp(steps), extent[dim] // blocks).reshape((-1,) + (1,) * (len(extent) - 1 - dim))
    return factor_of


def normal_values(stream_key, shape, scale, most, split=(), held_as=jnp.bfloat16):
    values = jax.random.normal(stream_key, shape, jnp.float32) * scale
    if len(split) > 0:
        values = level_of(stream_key, shape, split, -0.22, 0.18) * values
    return jnp.clip(values, min=-most, max=most).astype(held_as)


def setup_inputs(seed: int = 0) -> dict:
    streams_of = jax.random.split(jax.random.key(seed), 12)
    return {
        "positions": draw_positions(jax.random.fold_in(streams_of[11], 71), 0),
        "velocities": normal_values(streams_of[1], (NSB, NTB, 3, 128), 0.5, 3.0, ((0, 16), (1, 16)), jnp.float32),
        "features": normal_values(streams_of[2], (NSB, NTB, COMP * CH, 128), 1.0, 6.0, ((0, 16), (1, 16))),
        "neighbours": draw_neighbours(jax.random.fold_in(streams_of[11], 71), 0),
        "counts": draw_counts(jax.random.fold_in(streams_of[11], 71), 0),
        "w_first": normal_values(streams_of[5], (RH, NB), NB ** -0.5, 2.0, (), jnp.float32),
        "w_second": normal_values(streams_of[6], (3 * CH, RH), RH ** -0.5, 0.75, (), jnp.float32),
        "w_read": normal_values(streams_of[7], (EH, 3 * CH), (3 * CH) ** -0.5, 0.4375, (), jnp.float32),
        "w_out": normal_values(streams_of[8], (EH,), EH ** -0.5, 0.5, (), jnp.float32),
        "fresh_positions": draw_fresh_positions(jax.random.fold_in(streams_of[11], 71), 0),
        "fresh_velocities": normal_values(streams_of[10], (NTB, 3, 128), 0.5, 3.0, ((0, 16),), jnp.float32),
    }


CUTOFF_RADIUS = 9.5
BLOCK_LENGTH = 13.2
KICK_FACTOR = 4.0
MOVE_FACTOR = 0.5
HIGHEST_MODE = lax.Precision.HIGHEST

def block_energy(window_pos, window_feat, slot_codes, live_count, w_first, w_second, w_read, w_out):
    channels = w_second.shape[0] // 3
    basis_count = w_first.shape[1]
    neighbors = slot_codes.shape[0]
    window_slot = slot_codes % 1152
    image_z = (slot_codes // 1152 - 1).astype(jnp.float32)
    near_block = window_slot // 128
    shock_shift = (near_block // 3 - 1).astype(jnp.float32)
    trans_shift = (near_block % 3 - 1).astype(jnp.float32)
    offsets = jnp.stack([shock_shift, trans_shift, image_z]) * BLOCK_LENGTH
    centre = window_pos[:, 512:640]
    others = jnp.take(window_pos, window_slot, axis=1)
    displace = others + offsets - centre[:, None, :]
    distance = jnp.sqrt(lax.optimization_barrier(jnp.sum(displace * displace, axis=0)))
    heading = displace / distance[None]
    ratio = distance / CUTOFF_RADIUS
    envelope = 1.0 - 28.0 * ratio ** 6 + 48.0 * ratio ** 7 - 21.0 * ratio ** 8
    freqs = math.pi / CUTOFF_RADIUS * jnp.arange(1, basis_count + 1).astype(jnp.float32)
    basis = math.sqrt(2.0 / CUTOFF_RADIUS) * jnp.sin(freqs[:, None, None] * distance[None]) / distance[None]
    slot_rank = lax.broadcasted_iota(jnp.int32, slot_codes.shape, 0)
    live = (slot_rank < live_count[None, :]).astype(jnp.float32)
    hidden = jax.nn.silu(jnp.dot(w_first, basis.reshape(basis_count, -1), precision=HIGHEST_MODE))
    radial = jnp.dot(w_second, hidden, precision=HIGHEST_MODE).reshape(3, channels, neighbors, 128)
    radial = radial * (envelope * live)[None, None]
    unit_x, unit_y, unit_z = (heading[0], heading[1], heading[2])
    root_three = math.sqrt(3.0)
    root_fifteen = math.sqrt(15.0)
    root_five = math.sqrt(5.0)
    harmonics = jnp.stack([jnp.ones_like(unit_x), root_three * unit_x, root_three * unit_y, root_three * unit_z, root_fifteen * unit_x * unit_y, root_fifteen * unit_y * unit_z, 0.5 * root_five * (3.0 * unit_z * unit_z - 1.0), root_fifteen * unit_x * unit_z, 0.5 * root_fifteen * (unit_x * unit_x - unit_y * unit_y)])
    gathered = jnp.take(window_feat, window_slot, axis=1).reshape(9, channels, neighbors, 128).astype(jnp.float32)
    along = jnp.einsum('cna,mna->mca', radial[0] * gathered[0], harmonics, precision=HIGHEST_MODE)
    direct = lax.optimization_barrier(jnp.sum(radial[1][None] * gathered, axis=2))
    vector_dot = lax.optimization_barrier(jnp.sum(gathered[1:4] * harmonics[1:4][:, None], axis=0))
    coupled = lax.optimization_barrier(jnp.sum(radial[2] * vector_dot, axis=1))
    tensor_sum = (along + direct).at[0].add(coupled) / neighbors
    squares = tensor_sum * tensor_sum
    invariants = jnp.concatenate([squares[0], lax.optimization_barrier(jnp.sum(squares[1:4], axis=0)), lax.optimization_barrier(jnp.sum(squares[4:9], axis=0))], axis=0)
    readout = jax.nn.silu(jnp.dot(w_read, invariants, precision=HIGHEST_MODE))
    return jnp.dot(w_out, readout, precision=HIGHEST_MODE)

def take_window(extended, row, col):
    zero = jnp.zeros((), jnp.int32)
    piece = lax.dynamic_slice(extended, (row, col, zero, zero), (3, 3, extended.shape[2], 128))
    return jnp.moveaxis(piece, 2, 0).reshape(extended.shape[2], 1152)

def sweep(pos_ext, feat_ext, neighbours, counts, w_first, w_second, w_read, w_out):
    nrows, ncols = (neighbours.shape[0], neighbours.shape[1])
    zero = jnp.zeros((), jnp.int32)

    def visit(block_id, carry):
        forces, energies = carry
        row = (block_id // ncols).astype(jnp.int32)
        col = (block_id % ncols).astype(jnp.int32)
        window_pos = take_window(pos_ext, row, col)
        window_feat = take_window(feat_ext, row, col)
        slot_codes = lax.dynamic_slice(neighbours, (row, col, zero, zero), (1, 1, neighbours.shape[2], 128))[0, 0]
        live_count = lax.dynamic_slice(counts, (row, col, zero), (1, 1, 128))[0, 0]

        def energy_of(place):
            return block_energy(place, window_feat, slot_codes, live_count, w_first, w_second, w_read, w_out)
        energy, pullback = jax.vjp(energy_of, window_pos)
        grad = pullback(jnp.ones_like(energy))[0]
        piece = jnp.moveaxis(grad.reshape(3, 3, 3, 128), 0, 2)
        current = lax.dynamic_slice(forces, (row, col, zero, zero), (3, 3, 3, 128))
        forces = lax.dynamic_update_slice(forces, current - piece, (row, col, zero, zero))
        energies = lax.dynamic_update_slice(energies, energy[None, None], (row, col, zero))
        return (forces, energies)
    start = (jnp.zeros(pos_ext.shape, jnp.float32), jnp.zeros((nrows, ncols, 128), jnp.float32))
    return lax.fori_loop(0, nrows * ncols, visit, start)

def extend(values):
    wrapped = jnp.concatenate([values[:, -1:], values, values[:, :1]], axis=1)
    return jnp.pad(wrapped, ((1, 1), (0, 0), (0, 0), (0, 0)))

def reference(positions, velocities, features, neighbours, counts, w_first, w_second, w_read, w_out, fresh_positions, fresh_velocities):
    pos_ext = extend(positions)
    feat_ext = extend(features)
    forces_ext, energies = sweep(pos_ext, feat_ext, neighbours, counts, w_first, w_second, w_read, w_out)
    ncols = positions.shape[1]
    inner = forces_ext[1:-1]
    folded = inner[:, 1:ncols + 1]
    folded = folded.at[:, ncols - 1].add(inner[:, 0])
    folded = folded.at[:, 0].add(inner[:, ncols + 1])
    new_vel = velocities + KICK_FACTOR * folded
    moved = positions + MOVE_FACTOR * new_vel
    new_positions = jnp.concatenate([moved[1:], fresh_positions[None]], axis=0)
    new_velocities = jnp.concatenate([new_vel[1:], fresh_velocities[None]], axis=0)
    return (energies, new_positions, new_velocities)
```

```python
import math

import jax
import jax.numpy as jnp
from jax import lax
from jax.experimental import pallas as pl
from jax.experimental.pallas import tpu as pltpu

CUTOFF_RADIUS = 9.5
BLOCK_LENGTH = 13.2
KICK_FACTOR = 4.0
MOVE_FACTOR = 0.5
F32 = jnp.float32
BF16 = jnp.bfloat16
GEO = 12
SPAN = 4


def split(x):
    hi = x.astype(BF16)
    return hi, (x - hi.astype(F32)).astype(BF16)


def sigmoid(z):
    return 0.5 * jnp.tanh(0.5 * z) + 0.5


def sin_cos_pi(t):
    whole = jnp.floor(t + 0.5)
    half = whole * 0.5
    sign = 1.0 - 4.0 * (half - jnp.floor(half))
    r = (t - whole) * math.pi
    r2 = r * r
    s = r * (1.0 + r2 * (-1 / 6 + r2 * (1 / 120 + r2 * (-1 / 5040 + r2 * (1 / 362880 - r2 / 39916800)))))
    c = 1.0 + r2 * (
        -1 / 2 + r2 * (1 / 24 + r2 * (-1 / 720 + r2 * (1 / 40320 + r2 * (-1 / 3628800 + r2 / 479001600))))
    )
    return s * sign, c * sign


def geometry(r, pos, codes, counts, geo, unit):
    for part in range(3):
        rows = slice(8 * part, 8 * part + 8)
        code = codes[r, 0, rows, :]
        j = code & 127
        cell = code >> 7
        iz = (cell >= 9).astype(jnp.int32) + (cell >= 18).astype(jnp.int32)
        k = cell - 9 * iz
        is_ = (k >= 3).astype(jnp.int32) + (k >= 6).astype(jnp.int32)
        it = k - 3 * is_
        shifts = [(v - 1).astype(F32) * BLOCK_LENGTH for v in (is_, it, iz)]
        delta = []
        for comp in range(3):
            other = jnp.zeros((8, 128), F32)
            for b in range(9):
                row = pos[r + b // 3, b % 3, pl.ds(comp, 8, stride=0), :]
                got = jnp.take_along_axis(row, j, axis=1, mode="promise_in_bounds")
                other = jnp.where(k == b, got, other)
            centre = pos[r + 1, 1, pl.ds(comp, 8, stride=0), :]
            delta.append(other + shifts[comp] - centre)
        dx, dy, dz = delta
        d = jnp.sqrt(dx * dx + dy * dy + dz * dz)
        rinv = 1.0 / d
        ux, uy, uz = dx * rinv, dy * rinv, dz * rinv
        x = d * (1.0 / CUTOFF_RADIUS)
        x2 = x * x
        x4 = x2 * x2
        slot = lax.broadcasted_iota(jnp.int32, (8, 128), 0) + 8 * part
        live = jnp.where(slot < counts[pl.ds(r, 8, stride=0), :], 1.0 / 24.0, 0.0)
        env = (1.0 + x4 * x2 * (-28.0 + x * (48.0 - 21.0 * x))) * live
        slope = (-168.0 / CUTOFF_RADIUS) * x4 * x * ((1.0 - x) * (1.0 - x)) * live
        r3, r5, r15 = math.sqrt(3.0), math.sqrt(5.0), math.sqrt(15.0)
        values = [
            r3 * ux,
            r3 * uy,
            r3 * uz,
            r15 * ux * uy,
            r15 * uy * uz,
            0.5 * r5 * (3.0 * uz * uz - 1.0),
            r15 * ux * uz,
            0.5 * r15 * (ux * ux - uy * uy),
            x,
            rinv,
            env,
            slope,
        ]
        for q, v in enumerate(values):
            geo[r, q, rows, :] = v
        for q, v in enumerate((ux, uy, uz)):
            unit[r, q, rows, :] = v


def radial(step, geo, first, second, basis, hid, wgt):
    per = 24 // SPAN
    r = step // per
    n0 = (step % per) * SPAN
    order = (lax.broadcasted_iota(jnp.int32, (8, 128), 0) + 1).astype(F32)
    scale = math.sqrt(2.0 / CUTOFF_RADIUS)
    zero8 = jnp.zeros((8, 128), F32)
    for q in range(SPAN):
        x = geo[r, 8, pl.ds(n0 + q, 8, stride=0), :]
        rinv = geo[r, 9, pl.ds(n0 + q, 8, stride=0), :]
        s, c = sin_cos_pi(x * order)
        b = (scale * rinv) * s
        bd = rinv * ((scale * math.pi / CUTOFF_RADIUS) * order * c - b)
        for v, at in ((b, q), (bd, SPAN + q)):
            hi = v.astype(BF16).astype(F32)
            lanes = slice(128 * at, 128 * at + 128)
            basis[0:16, lanes] = jnp.concatenate([hi, v - hi], axis=0).astype(BF16)
            basis[16:32, lanes] = jnp.concatenate([hi, zero8], axis=0).astype(BF16)
    z = jnp.dot(first, basis[...], preferred_element_type=F32)
    for q in range(SPAN):
        env = geo[r, 10, pl.ds(n0 + q, 8, stride=0), :]
        slope = geo[r, 11, pl.ds(n0 + q, 8, stride=0), :]
        env, slope = (jnp.concatenate([v] * 8, axis=0) for v in (env, slope))
        zq = z[:, 128 * q : 128 * q + 128]
        zd = z[:, 128 * (SPAN + q) : 128 * (SPAN + q) + 128]
        sig = sigmoid(zq)
        act = zq * sig
        h = act * env
        hd = (sig + act * (1.0 - sig)) * zd * env + act * slope
        for v, at in ((h, q), (hd, SPAN + q)):
            hi, lo = split(v)
            lanes = slice(128 * at, 128 * at + 128)
            hid[0:64, lanes] = hi
            hid[64:128, lanes] = lo
            hid[128:192, lanes] = hi
    w = jnp.dot(second, hid[...], preferred_element_type=F32)
    for q in range(SPAN):
        wgt[r, n0 + q, 0] = w[:, 128 * q : 128 * q + 128]
        wgt[r, n0 + q, 1] = w[:, 128 * (SPAN + q) : 128 * (SPAN + q) + 128]


def gather(step, codes, window, got):
    r = step // 12
    n0 = (step % 12) * 2
    ids = lax.broadcasted_iota(jnp.int32, (128, 128), 0).astype(F32).astype(BF16)
    halves = []
    for q in range(2):
        code = codes[r, 0, pl.ds(n0 + q, 16, stride=0), :]
        j = (code & 127).astype(F32)
        cell = code >> 7
        k = cell - 9 * ((cell >= 9).astype(jnp.int32) + (cell >= 18).astype(jnp.int32))
        pieces = []
        for b in range(9):
            val = jnp.where(k == b, j, -1.0).astype(BF16)
            val = jnp.concatenate([val] * 8, axis=0)
            pieces.append(jnp.where(val == ids, jnp.ones((), BF16), jnp.zeros((), BF16)))
        halves.append(jnp.concatenate(pieces, axis=0))
    hot = jnp.concatenate(halves, axis=1)
    out = jnp.dot(window[r], hot, preferred_element_type=F32)
    got[r, n0] = out[:, :128]
    got[r, n0 + 1] = out[:, 128:]


def row8(ref, r, q, n, times=1):
    v = ref[r, q, pl.ds(n, 8, stride=0), :]
    return v if times == 1 else jnp.concatenate([v] * times, axis=0)


TILE = 16


def aggregate(step, geo, wgt, got, agg):
    per = 64 // TILE
    r = step // per
    c0 = pl.multiple_of((step % per) * TILE, TILE)

    def body(n, acc):
        acc = list(acc)
        y = [None] + [row8(geo, r, q, n, TILE // 8) for q in range(8)]
        x = [got[r, n, pl.ds(m * 64 + c0, TILE), :] for m in range(9)]
        w = [wgt[r, n, 0, pl.ds(p * 64 + c0, TILE), :] for p in range(3)]
        p0 = w[0] * x[0]
        v = x[1] * y[1] + x[2] * y[2] + x[3] * y[3]
        acc[0] += p0 + w[1] * x[0] + w[2] * v
        for m in range(1, 9):
            acc[m] += p0 * y[m] + w[1] * x[m]
        return tuple(acc)

    acc = lax.fori_loop(0, 24, body, (jnp.zeros((TILE, 128), F32),) * 9, unroll=4)
    for m in range(9):
        agg[r, m, pl.ds(c0, TILE), :] = acc[m]


def readout(agg, read3, read_t3, w_out, energies):
    inv = []
    for r in range(2):
        a = [agg[r, m] for m in range(9)]
        sq = [v * v for v in a]
        inv.append(
            jnp.concatenate(
                [sq[0], sq[1] + sq[2] + sq[3], sq[4] + sq[5] + sq[6] + sq[7] + sq[8]], axis=0
            )
        )
    s = jnp.concatenate(inv, axis=1)
    hi, lo = split(s)
    z = jnp.dot(read3, jnp.concatenate([hi, lo, hi], axis=0), preferred_element_type=F32)
    sig = sigmoid(z)
    act = z * sig
    energy = jnp.sum(w_out * act, axis=0, keepdims=True)
    energies[0:1, :] = energy[:, :128]
    energies[1:2, :] = energy[:, 128:]
    gz = w_out * (sig + act * (1.0 - sig))
    hi, lo = split(gz)
    gs = jnp.dot(read_t3, jnp.concatenate([hi, lo, hi], axis=0), preferred_element_type=F32)
    gs = gs + gs
    for r in range(2):
        g = gs[:, 128 * r : 128 * r + 128]
        for m in range(9):
            part = 0 if m == 0 else 1 if m < 4 else 2
            agg[r, m] = agg[r, m] * g[64 * part : 64 * part + 64]


def backward(step, geo, wgt, got, agg, slopes):
    r = step // 24
    n = step % 24
    y = [None] + [row8(geo, r, q, n) for q in range(8)]
    acc = [jnp.zeros((8, 128), F32)] * 9
    for c in range(8):
        x = [got[r, n, m * 64 + 8 * c : m * 64 + 8 * c + 8, :] for m in range(9)]
        g = [agg[r, m, 8 * c : 8 * c + 8, :] for m in range(9)]
        w0, _, w2 = [wgt[r, n, 0, p * 64 + 8 * c : p * 64 + 8 * c + 8, :] for p in range(3)]
        d0, d1, d2 = [wgt[r, n, 1, p * 64 + 8 * c : p * 64 + 8 * c + 8, :] for p in range(3)]
        gx = g[0] * x[0]
        gy = g[0]
        for m in range(1, 9):
            gx += g[m] * x[m]
            gy += g[m] * y[m]
        v = x[1] * y[1] + x[2] * y[2] + x[3] * y[3]
        acc[0] += d1 * gx + d0 * (gy * x[0]) + d2 * (g[0] * v)
        p0 = w0 * x[0]
        p2 = w2 * g[0]
        for m in range(1, 9):
            acc[m] += p0 * g[m] + p2 * x[m] if m < 4 else p0 * g[m]
    for q in range(9):
        slopes[r, q, pl.ds(n, 1), :] = jnp.sum(acc[q], axis=0, keepdims=True)


def edge_forces(r, geo, unit, slopes, edge):
    r3, r5, r15 = math.sqrt(3.0), math.sqrt(5.0), math.sqrt(15.0)
    ux, uy, uz = (unit[r, q] for q in range(3))
    rinv = geo[r, 9]
    gd, g1, g2, g3, g4, g5, g6, g7, g8 = (slopes[r, q] for q in range(9))
    gx = r3 * g1 + r15 * (uy * g4 + uz * g7 + ux * g8)
    gy = r3 * g2 + r15 * (ux * g4 + uz * g5 - uy * g8)
    gz = r3 * g3 + r15 * (uy * g5 + ux * g7) + (3.0 * r5) * uz * g6
    along = gd - (gx * ux + gy * uy + gz * uz) * rinv
    out = []
    for q, (g, u) in enumerate(((gx, ux), (gy, uy), (gz, uz))):
        f = g * rinv + along * u
        edge[q] = f
        out.append(jnp.sum(f, axis=0, keepdims=True))
    return out


def scatter(r, codes, edge, lhs, hot, centre, forces):
    ids = lax.broadcasted_iota(jnp.int32, (128, 128), 0).astype(F32).astype(BF16)
    pick = lax.broadcasted_iota(jnp.int32, (8, 128), 0)

    def body(n, carry):
        code = codes[r, 0, pl.ds(n, 8, stride=0), :]
        cell = code >> 7
        k = cell - 9 * ((cell >= 9).astype(jnp.int32) + (cell >= 18).astype(jnp.int32))
        value = jnp.zeros((8, 128), F32)
        for q in range(3):
            f = edge[q, pl.ds(n, 8, stride=0), :]
            hi = f.astype(BF16).astype(F32)
            value = jnp.where(pick == q, hi, jnp.where(pick == q + 3, f - hi, value))
        rows = [jnp.where(k == b, value, 0.0) for b in range(9)] + [jnp.zeros((8, 128), F32)]
        lanes = pl.ds(pl.multiple_of(n * 128, 128), 128)
        lhs[:, lanes] = jnp.concatenate(rows, axis=0).astype(BF16)
        j = (codes[r, 0, pl.ds(n, 16, stride=0), :] & 127).astype(F32).astype(BF16)
        j = jnp.concatenate([j] * 8, axis=0)
        hot[:, lanes] = jnp.where(j == ids, jnp.ones((), BF16), jnp.zeros((), BF16))
        return carry

    lax.fori_loop(0, 24, body, 0, unroll=2)
    out = lax.dot_general(lhs[...], hot[...], (((1,), (1,)), ((), ())), preferred_element_type=F32)
    for b in range(9):
        at = (r + b // 3, b % 3)
        for q in range(3):
            v = -(out[8 * b + q : 8 * b + q + 1] + out[8 * b + q + 3 : 8 * b + q + 4])
            if b == 4:
                v += centre[q]
            forces[at[0], at[1], q : q + 1, :] += v


def split_whole(w):
    rounded = lax.reduce_precision(w, 8, 7)
    return rounded.astype(BF16), (w - rounded).astype(BF16)


def stack3(w):
    hi, lo = split_whole(w)
    return jnp.concatenate([hi, hi, lo], axis=1)


def block_kernel(
    pos, feat, codes, counts, w_first, w_second, w_read, w_read_t, w_out, energies, forces,
    geo, unit, basis, hid, wgt, window, got, agg, slopes, edge, lhs, hot,
):
    for r in range(2):
        geometry(r, pos, codes, counts, geo, unit)
        for b in range(9):
            window[r, :, 128 * b : 128 * b + 128] = feat[r + b // 3, b % 3]

    def radial_step(step, carry):
        radial(step, geo, w_first[...], w_second[...], basis, hid, wgt)
        return carry

    lax.fori_loop(0, 48 // SPAN, radial_step, 0)

    def gather_step(step, carry):
        gather(step, codes, window, got)
        return carry

    lax.fori_loop(0, 24, gather_step, 0)

    def aggregate_step(step, carry):
        aggregate(step, geo, wgt, got, agg)
        return carry

    lax.fori_loop(0, 2 * (64 // TILE), aggregate_step, 0)
    readout(agg, w_read[...], w_read_t[...], w_out[...], energies)

    def backward_step(step, carry):
        backward(step, geo, wgt, got, agg, slopes)
        return carry

    lax.fori_loop(0, 48, backward_step, 0)
    forces[...] = jnp.zeros_like(forces)
    for r in range(2):
        centre = edge_forces(r, geo, unit, slopes, edge)
        scatter(r, codes, edge, lhs, hot, centre, forces)


def weights(w_first, w_second, w_read, w_out):
    hi, lo = split_whole(w_first)
    first = jnp.concatenate([hi, hi, lo, jnp.zeros_like(hi)], axis=1)
    out = jnp.broadcast_to(w_out[:, None], (w_out.shape[0], 256))
    return first, stack3(w_second), stack3(w_read), stack3(w_read.T), out


def blocks(pos_ext, feat_ext, codes, counts, w):
    vmem = pl.BlockSpec(memory_space=pltpu.VMEM)
    return pl.pallas_call(
        block_kernel,
        out_shape=(
            jax.ShapeDtypeStruct((2, 128), F32),
            jax.ShapeDtypeStruct((4, 3, 3, 128), F32),
        ),
        in_specs=[vmem] * 9,
        out_specs=(vmem, vmem),
        scratch_shapes=[
            pltpu.VMEM((2, GEO, 24, 128), F32),
            pltpu.VMEM((2, 3, 24, 128), F32),
            pltpu.VMEM((32, 256 * SPAN), BF16),
            pltpu.VMEM((192, 256 * SPAN), BF16),
            pltpu.VMEM((2, 24, 2, 192, 128), F32),
            pltpu.VMEM((2, 576, 1152), BF16),
            pltpu.VMEM((2, 24, 576, 128), F32),
            pltpu.VMEM((2, 9, 64, 128), F32),
            pltpu.VMEM((2, 9, 24, 128), F32),
            pltpu.VMEM((3, 24, 128), F32),
            pltpu.VMEM((80, 3072), BF16),
            pltpu.VMEM((128, 3072), BF16),
        ],
        compiler_params=pltpu.CompilerParams(vmem_limit_bytes=56 << 20),
        name="blocks",
    )(pos_ext, feat_ext, codes, counts, *w)
from jax.sharding import PartitionSpec as P


def extended_2(x, sides, width):
    for axis, dim in sides:
        count, length = (lax.axis_size(axis), x.shape[dim])
        up = [(i, (i + 1) % count) for i in range(count)]
        down = [(j, i) for i, j in up]
        last = lax.slice_in_dim(x, length - width, length, axis=dim)
        first = lax.slice_in_dim(x, 0, width, axis=dim)
        before = lax.ppermute(last, axis, up)
        after = lax.ppermute(first, axis, down)
        x = jnp.concatenate([before, x, after], axis=dim)
    return x


def shifted(x, axis, by):
    count = lax.axis_size(axis)
    return lax.ppermute(x, axis, [(i, (i + by) % count) for i in range(count)])


def passed_along(block, axis, distance):
    devices = range(lax.axis_size(axis))
    route = [(i - distance, i) for i in devices if i - distance in devices]
    return lax.ppermute(block, axis, route)


def local(
    positions, velocities, features, neighbours, counts, w_first, w_second, w_read, w_out,
    fresh_positions, fresh_velocities,
):
    nrows, ncols = (positions.shape[0], positions.shape[1])
    shock_place = lax.axis_index("shock")
    front = lax.axis_size("shock") - 1
    pos_ext = extended_2(positions, (("trans", 1), ("shock", 0)), 1)
    feat_ext = extended_2(features, (("trans", 1), ("shock", 0)), 1)
    ext_rows = lax.broadcasted_iota(jnp.int32, (nrows + 2, 1, 1, 1), 0)
    outside = (ext_rows == 0) & (shock_place == 0) | (ext_rows == nrows + 1) & (
        shock_place == front
    )
    pos_ext = jnp.where(outside, jnp.zeros((), jnp.float32), pos_ext)
    feat_ext = jnp.where(outside, jnp.zeros((), jnp.bfloat16), feat_ext)
    energies, forces_ext = blocks(
        pos_ext, feat_ext, neighbours, counts[:, 0], weights(w_first, w_second, w_read, w_out)
    )
    from_right = shifted(forces_ext[:, 0], "trans", -1)
    from_left = shifted(forces_ext[:, ncols + 1], "trans", 1)
    folded = forces_ext[:, 1 : ncols + 1]
    folded = folded.at[:, ncols - 1].add(from_right)
    folded = folded.at[:, 0].add(from_left)
    partial_force = folded[1 : nrows + 1]
    from_front = passed_along(folded[0], "shock", -1)
    from_rear = passed_along(folded[nrows + 1], "shock", 1)
    total_force = partial_force.at[nrows - 1].add(from_front)
    total_force = total_force.at[0].add(from_rear)
    new_vel = velocities + KICK_FACTOR * total_force
    moved = positions + MOVE_FACTOR * new_vel
    incoming_pos, incoming_vel = passed_along((moved[0], new_vel[0]), "shock", -1)
    at_front = shock_place == front
    last_pos = jnp.where(at_front, fresh_positions, incoming_pos)
    last_vel = jnp.where(at_front, fresh_velocities, incoming_vel)
    new_positions = jnp.concatenate([moved[1:], last_pos[None]], axis=0)
    new_velocities = jnp.concatenate([new_vel[1:], last_vel[None]], axis=0)
    return (energies[:, None], new_positions, new_velocities)


def solution(mesh):
    spec = P("shock", "trans", None, None)
    return jax.shard_map(
        local,
        mesh=mesh,
        in_specs=(
            spec, spec, spec, spec, P("shock", "trans", None), P(), P(), P(), P(),
            P("trans", None, None), P("trans", None, None),
        ),
        out_specs=(P("shock", "trans", None), spec, spec),
        check_vma=False,
    )
```

```python
import math

import jax
import jax.numpy as jnp
from jax import lax
from jax.experimental import pallas as pl
from jax.experimental.pallas import tpu as pltpu
from jax.sharding import PartitionSpec as P

CUTOFF_RADIUS = 9.5
BLOCK_LENGTH = 13.2
KICK_FACTOR = 4.0
MOVE_FACTOR = 0.5
F32 = jnp.float32
BF16 = jnp.bfloat16
GEO = 12
SPAN = 4


def split(x):
    hi = x.astype(BF16)
    return hi, (x - hi.astype(F32)).astype(BF16)


def sigmoid(z):
    return 0.5 * jnp.tanh(0.5 * z) + 0.5


def sin_cos_pi(t):
    whole = jnp.floor(t + 0.5)
    half = whole * 0.5
    sign = 1.0 - 4.0 * (half - jnp.floor(half))
    r = (t - whole) * math.pi
    r2 = r * r
    s = r * (1.0 + r2 * (-1 / 6 + r2 * (1 / 120 + r2 * (-1 / 5040 + r2 * (1 / 362880 - r2 / 39916800)))))
    c = 1.0 + r2 * (
        -1 / 2 + r2 * (1 / 24 + r2 * (-1 / 720 + r2 * (1 / 40320 + r2 * (-1 / 3628800 + r2 / 479001600))))
    )
    return s * sign, c * sign


def geometry(r, pos, codes, counts, geo, unit):
    for part in range(3):
        rows = slice(8 * part, 8 * part + 8)
        code = codes[r, 0, rows, :]
        j = code & 127
        cell = code >> 7
        iz = (cell >= 9).astype(jnp.int32) + (cell >= 18).astype(jnp.int32)
        k = cell - 9 * iz
        is_ = (k >= 3).astype(jnp.int32) + (k >= 6).astype(jnp.int32)
        it = k - 3 * is_
        shifts = [(v - 1).astype(F32) * BLOCK_LENGTH for v in (is_, it, iz)]
        delta = []
        for comp in range(3):
            other = jnp.zeros((8, 128), F32)
            for b in range(9):
                row = pos[r + b // 3, b % 3, pl.ds(comp, 8, stride=0), :]
                got = jnp.take_along_axis(row, j, axis=1, mode="promise_in_bounds")
                other = jnp.where(k == b, got, other)
            centre = pos[r + 1, 1, pl.ds(comp, 8, stride=0), :]
            delta.append(other + shifts[comp] - centre)
        dx, dy, dz = delta
        d = jnp.sqrt(dx * dx + dy * dy + dz * dz)
        rinv = 1.0 / d
        ux, uy, uz = dx * rinv, dy * rinv, dz * rinv
        x = d * (1.0 / CUTOFF_RADIUS)
        x2 = x * x
        x4 = x2 * x2
        slot = lax.broadcasted_iota(jnp.int32, (8, 128), 0) + 8 * part
        live = jnp.where(slot < counts[r, pl.ds(0, 8, stride=0), :], 1.0 / 24.0, 0.0)
        env = (1.0 + x4 * x2 * (-28.0 + x * (48.0 - 21.0 * x))) * live
        slope = (-168.0 / CUTOFF_RADIUS) * x4 * x * ((1.0 - x) * (1.0 - x)) * live
        r3, r5, r15 = math.sqrt(3.0), math.sqrt(5.0), math.sqrt(15.0)
        values = [
            r3 * ux,
            r3 * uy,
            r3 * uz,
            r15 * ux * uy,
            r15 * uy * uz,
            0.5 * r5 * (3.0 * uz * uz - 1.0),
            r15 * ux * uz,
            0.5 * r15 * (ux * ux - uy * uy),
            x,
            rinv,
            env,
            slope,
        ]
        for q, v in enumerate(values):
            geo[r, q, rows, :] = v
        for q, v in enumerate((ux, uy, uz)):
            unit[r, q, rows, :] = v


def radial(step, geo, first, second, basis, hid, wgt):
    per = 24 // SPAN
    r = step // per
    n0 = (step % per) * SPAN
    order = (lax.broadcasted_iota(jnp.int32, (8, 128), 0) + 1).astype(F32)
    scale = math.sqrt(2.0 / CUTOFF_RADIUS)
    zero8 = jnp.zeros((8, 128), F32)
    for q in range(SPAN):
        x = geo[r, 8, pl.ds(n0 + q, 8, stride=0), :]
        rinv = geo[r, 9, pl.ds(n0 + q, 8, stride=0), :]
        s, c = sin_cos_pi(x * order)
        b = (scale * rinv) * s
        bd = rinv * ((scale * math.pi / CUTOFF_RADIUS) * order * c - b)
        for v, at in ((b, q), (bd, SPAN + q)):
            hi = v.astype(BF16).astype(F32)
            lanes = slice(128 * at, 128 * at + 128)
            basis[0:16, lanes] = jnp.concatenate([hi, v - hi], axis=0).astype(BF16)
            basis[16:32, lanes] = jnp.concatenate([hi, zero8], axis=0).astype(BF16)
    z = jnp.dot(first, basis[...], preferred_element_type=F32)
    for q in range(SPAN):
        env = geo[r, 10, pl.ds(n0 + q, 8, stride=0), :]
        slope = geo[r, 11, pl.ds(n0 + q, 8, stride=0), :]
        env, slope = (jnp.concatenate([v] * 8, axis=0) for v in (env, slope))
        zq = z[:, 128 * q : 128 * q + 128]
        zd = z[:, 128 * (SPAN + q) : 128 * (SPAN + q) + 128]
        sig = sigmoid(zq)
        act = zq * sig
        h = act * env
        hd = (sig + act * (1.0 - sig)) * zd * env + act * slope
        for v, at in ((h, q), (hd, SPAN + q)):
            hi, lo = split(v)
            lanes = slice(128 * at, 128 * at + 128)
            hid[0:64, lanes] = hi
            hid[64:128, lanes] = lo
            hid[128:192, lanes] = hi
    w = jnp.dot(second, hid[...], preferred_element_type=F32)
    for q in range(SPAN):
        wgt[r, n0 + q, 0] = w[:, 128 * q : 128 * q + 128]
        wgt[r, n0 + q, 1] = w[:, 128 * (SPAN + q) : 128 * (SPAN + q) + 128]


def gather(step, codes, window, got):
    r = step // 12
    n0 = (step % 12) * 2
    ids = lax.broadcasted_iota(jnp.int32, (128, 128), 0).astype(F32).astype(BF16)
    halves = []
    for q in range(2):
        code = codes[r, 0, pl.ds(n0 + q, 16, stride=0), :]
        j = (code & 127).astype(F32)
        cell = code >> 7
        k = cell - 9 * ((cell >= 9).astype(jnp.int32) + (cell >= 18).astype(jnp.int32))
        pieces = []
        for b in range(9):
            val = jnp.where(k == b, j, -1.0).astype(BF16)
            val = jnp.concatenate([val] * 8, axis=0)
            pieces.append(jnp.where(val == ids, jnp.ones((), BF16), jnp.zeros((), BF16)))
        halves.append(jnp.concatenate(pieces, axis=0))
    hot = jnp.concatenate(halves, axis=1)
    out = jnp.dot(window[r], hot, preferred_element_type=F32)
    got[r, n0] = out[:, :128]
    got[r, n0 + 1] = out[:, 128:]


def row8(ref, r, q, n, times=1):
    v = ref[r, q, pl.ds(n, 8, stride=0), :]
    return v if times == 1 else jnp.concatenate([v] * times, axis=0)


TILE = 16


def aggregate(step, geo, wgt, got, agg):
    per = 64 // TILE
    r = step // per
    c0 = pl.multiple_of((step % per) * TILE, TILE)

    def body(n, acc):
        acc = list(acc)
        y = [None] + [row8(geo, r, q, n, TILE // 8) for q in range(8)]
        x = [got[r, n, pl.ds(m * 64 + c0, TILE), :] for m in range(9)]
        w = [wgt[r, n, 0, pl.ds(p * 64 + c0, TILE), :] for p in range(3)]
        p0 = w[0] * x[0]
        v = x[1] * y[1] + x[2] * y[2] + x[3] * y[3]
        acc[0] += p0 + w[1] * x[0] + w[2] * v
        for m in range(1, 9):
            acc[m] += p0 * y[m] + w[1] * x[m]
        return tuple(acc)

    acc = lax.fori_loop(0, 24, body, (jnp.zeros((TILE, 128), F32),) * 9, unroll=4)
    for m in range(9):
        agg[r, m, pl.ds(c0, TILE), :] = acc[m]


def readout(agg, read3, read_t3, w_out, energies):
    inv = []
    for r in range(2):
        a = [agg[r, m] for m in range(9)]
        sq = [v * v for v in a]
        inv.append(
            jnp.concatenate(
                [sq[0], sq[1] + sq[2] + sq[3], sq[4] + sq[5] + sq[6] + sq[7] + sq[8]], axis=0
            )
        )
    s = jnp.concatenate(inv, axis=1)
    hi, lo = split(s)
    z = jnp.dot(read3, jnp.concatenate([hi, lo, hi], axis=0), preferred_element_type=F32)
    sig = sigmoid(z)
    act = z * sig
    energy = jnp.sum(w_out * act, axis=0, keepdims=True)
    energies[0] = energy[:, :128]
    energies[1] = energy[:, 128:]
    gz = w_out * (sig + act * (1.0 - sig))
    hi, lo = split(gz)
    gs = lax.dot_general(
        read_t3,
        jnp.concatenate([hi, lo, hi], axis=0),
        (((0,), (0,)), ((), ())),
        preferred_element_type=F32,
    )
    gs = gs + gs
    for r in range(2):
        g = gs[:, 128 * r : 128 * r + 128]
        for m in range(9):
            part = 0 if m == 0 else 1 if m < 4 else 2
            agg[r, m] = agg[r, m] * g[64 * part : 64 * part + 64]


def backward(step, geo, wgt, got, agg, slopes):
    r = step // 24
    n = step % 24
    y = [None] + [row8(geo, r, q, n) for q in range(8)]
    acc = [jnp.zeros((8, 128), F32)] * 9
    for c in range(8):
        x = [got[r, n, m * 64 + 8 * c : m * 64 + 8 * c + 8, :] for m in range(9)]
        g = [agg[r, m, 8 * c : 8 * c + 8, :] for m in range(9)]
        w0, _, w2 = [wgt[r, n, 0, p * 64 + 8 * c : p * 64 + 8 * c + 8, :] for p in range(3)]
        d0, d1, d2 = [wgt[r, n, 1, p * 64 + 8 * c : p * 64 + 8 * c + 8, :] for p in range(3)]
        gx = g[0] * x[0]
        gy = g[0]
        for m in range(1, 9):
            gx += g[m] * x[m]
            gy += g[m] * y[m]
        v = x[1] * y[1] + x[2] * y[2] + x[3] * y[3]
        acc[0] += d1 * gx + d0 * (gy * x[0]) + d2 * (g[0] * v)
        p0 = w0 * x[0]
        p2 = w2 * g[0]
        for m in range(1, 9):
            acc[m] += p0 * g[m] + p2 * x[m] if m < 4 else p0 * g[m]
    for q in range(9):
        slopes[r, q, pl.ds(n, 1), :] = jnp.sum(acc[q], axis=0, keepdims=True)


def edge_forces(r, geo, unit, slopes, edge):
    r3, r5, r15 = math.sqrt(3.0), math.sqrt(5.0), math.sqrt(15.0)
    ux, uy, uz = (unit[r, q] for q in range(3))
    rinv = geo[r, 9]
    gd, g1, g2, g3, g4, g5, g6, g7, g8 = (slopes[r, q] for q in range(9))
    gx = r3 * g1 + r15 * (uy * g4 + uz * g7 + ux * g8)
    gy = r3 * g2 + r15 * (ux * g4 + uz * g5 - uy * g8)
    gz = r3 * g3 + r15 * (uy * g5 + ux * g7) + (3.0 * r5) * uz * g6
    along = gd - (gx * ux + gy * uy + gz * uz) * rinv
    out = []
    for q, (g, u) in enumerate(((gx, ux), (gy, uy), (gz, uz))):
        f = g * rinv + along * u
        edge[q] = f
        out.append(jnp.sum(f, axis=0, keepdims=True))
    return out


def scatter(r, codes, edge, lhs, hot, centre, forces):
    ids = lax.broadcasted_iota(jnp.int32, (128, 128), 0).astype(F32).astype(BF16)
    pick = lax.broadcasted_iota(jnp.int32, (8, 128), 0)

    def body(n, carry):
        code = codes[r, 0, pl.ds(n, 8, stride=0), :]
        cell = code >> 7
        k = cell - 9 * ((cell >= 9).astype(jnp.int32) + (cell >= 18).astype(jnp.int32))
        value = jnp.zeros((8, 128), F32)
        for q in range(3):
            f = edge[q, pl.ds(n, 8, stride=0), :]
            hi = f.astype(BF16).astype(F32)
            value = jnp.where(pick == q, hi, jnp.where(pick == q + 3, f - hi, value))
        rows = [jnp.where(k == b, value, 0.0) for b in range(9)] + [jnp.zeros((8, 128), F32)]
        lanes = pl.ds(pl.multiple_of(n * 128, 128), 128)
        lhs[:, lanes] = jnp.concatenate(rows, axis=0).astype(BF16)
        j = (codes[r, 0, pl.ds(n, 16, stride=0), :] & 127).astype(F32).astype(BF16)
        j = jnp.concatenate([j] * 8, axis=0)
        hot[:, lanes] = jnp.where(j == ids, jnp.ones((), BF16), jnp.zeros((), BF16))
        return carry

    lax.fori_loop(0, 24, body, 0, unroll=2)
    out = lax.dot_general(lhs[...], hot[...], (((1,), (1,)), ((), ())), preferred_element_type=F32)
    for b in range(9):
        for q in range(3):
            v = -(out[8 * b + q : 8 * b + q + 1] + out[8 * b + q + 3 : 8 * b + q + 4])
            if b == 4:
                v += centre[q]
            forces[b % 3, r + b // 3, q : q + 1, :] += v


def stack(w, axis):
    hi, lo = split(w)
    return jnp.concatenate([hi, hi, lo], axis=axis)


POS = 0
VEL = 8
OWN = 9
CHIP = 11
OFF = 12
CORNER = 13
FAR = 14
NEAR_CHIP = 16
FAR_CHIP = 17
FAR_CORNER = 18
TAIL = 19
COPIES = 24
AROUND = ((-1, -1), (-1, 0), (-1, 1), (0, -1), (0, 1), (1, -1), (1, 0), (1, 1))
BACK = ((0, 1), (0, -1), (-1, 1), (-1, 0), (-1, -1))


def step_kernel(
    positions, velocities, features, codes, counts, w_first, w_second, w_read, w_out,
    fresh_pos, fresh_vel, energies, new_pos, new_vel,
    pos, vel_in, fx, geo, unit, basis, hid, wgt, window, got, agg, slopes, edge, lhs, hot,
    forces, tail, first, second, read3, read_t3, out_col, own_sem, send_sem, recv_sem,
):
    s = lax.axis_index("shock")
    t = lax.axis_index("trans")
    ns = lax.axis_size("shock")
    nt = lax.axis_size("trans")
    core = lax.rem(s, 2)
    way = 1 - 2 * lax.rem(t, 2)
    out_way = 2 * core - 1

    def at(ds, dt):
        return (lax.rem(s + ds + ns, ns), lax.rem(t + dt + nt, nt))

    def copy(k, src, dst, to):
        return pltpu.make_async_remote_copy(
            src_ref=src,
            dst_ref=dst,
            send_sem=send_sem.at[k],
            recv_sem=recv_sem.at[k],
            device_id=to,
            device_id_type=pl.DeviceIdType.MESH,
        )

    barrier = pltpu.get_barrier_semaphore()
    for ds, dt in AROUND + ((0, 2), (0, -2)):
        pl.semaphore_signal(
            barrier, inc=1, device_id=at(ds, dt), device_id_type=pl.DeviceIdType.MESH
        )
    own = pltpu.make_async_copy(features.at[:, 0], fx.at[pl.ds(1, 2), 1], own_sem)
    own.start()
    pos[1:3, 1] = positions[:, 0]
    pl.semaphore_wait(barrier, 10)

    flights = {}
    for i, (ds, dt) in enumerate(AROUND):
        if ds == 0:
            src, dst = positions.at[:, 0], pos.at[pl.ds(1, 2), 1 - dt]
        elif ds == 1:
            src, dst = positions.at[1, 0], pos.at[0, 1 - dt]
        else:
            src, dst = positions.at[0, 0], pos.at[3, 1 - dt]
        flights[POS + i] = copy(POS + i, src, dst, at(ds, dt))
    flights[VEL] = copy(VEL, velocities.at[0, 0], vel_in, at(-1, 0))
    near, far = 1 + way, 1 - way
    for i in range(2):
        flights[OWN + i] = copy(OWN + i, features.at[i, 0], fx.at[1 + i, far], at(0, way))
    chip_row, chip_ghost = 1 - core, 3 * core
    off_row, off_ghost = core, 3 * (1 - core)
    flights[CHIP] = copy(CHIP, features.at[chip_row, 0], fx.at[chip_ghost, 1], at(-out_way, 0))
    flights[OFF] = copy(OFF, features.at[off_row, 0], fx.at[off_ghost, 1], at(out_way, 0))
    flights[CORNER] = copy(
        CORNER, features.at[off_row, 0], fx.at[off_ghost, far], at(out_way, way)
    )
    for k in list(range(POS, POS + 8)) + [OWN, OWN + 1, CORNER, OFF, CHIP, VEL]:
        flights[k].start()
    my_chip_ghost, my_off_ghost = 3 * (1 - core), 3 * core
    for i in range(2):
        flights[FAR + i] = copy(
            FAR + i, fx.at[1 + i, near], fx.at[1 + i, far], at(0, 2 * way)
        )
    flights[FAR_CORNER] = copy(
        FAR_CORNER, fx.at[my_off_ghost, near], fx.at[my_off_ghost, far], at(0, 2 * way)
    )
    flights[NEAR_CHIP] = copy(
        NEAR_CHIP, fx.at[1 + chip_row, near], fx.at[chip_ghost, near], at(-out_way, 0)
    )
    flights[FAR_CHIP] = copy(
        FAR_CHIP, fx.at[1 + chip_row, far], fx.at[chip_ghost, far], at(-out_way, 0)
    )

    first[...] = jnp.concatenate([stack(w_first[...], 1), jnp.zeros((64, 8), BF16)], axis=1)
    second[...] = stack(w_second[...], 1)
    read3[...] = stack(w_read[...], 1)
    read_t3[...] = stack(w_read[...], 0)
    col = jnp.broadcast_to(w_out[...], (128, 128)).T
    out_col[...] = jnp.concatenate([col, col], axis=1)

    for k in range(POS, POS + 8):
        flights[k].wait_recv()

    @pl.when(s == 0)
    def _():
        pos[0] = jnp.zeros((3, 3, 128), F32)

    @pl.when(s == ns - 1)
    def _():
        pos[3] = jnp.zeros((3, 3, 128), F32)

    for r in range(2):
        geometry(r, pos, codes, counts, geo, unit)

    def radial_steps(lo, hi):
        def radial_step(step, carry):
            radial(step, geo, first[...], second[...], basis, hid, wgt)
            return carry

        lax.fori_loop(lo, hi, radial_step, 0)

    total = 48 // SPAN
    radial_steps(0, total // 4)
    for i in range(2):
        flights[OWN + i].wait_recv()
        flights[FAR + i].start()
    flights[NEAR_CHIP].start()
    radial_steps(total // 4, total // 2)
    flights[CORNER].wait_recv()
    flights[FAR_CORNER].start()
    radial_steps(total // 2, total)
    for i in range(2):
        flights[FAR + i].wait_recv()
    flights[FAR_CHIP].start()
    own.wait()
    for k in (CHIP, OFF, NEAR_CHIP, FAR_CORNER, FAR_CHIP, VEL):
        flights[k].wait_recv()
    for k in range(TAIL):
        flights[k].wait_send()

    @pl.when(s == 0)
    def _():
        fx[0] = jnp.zeros((3, 576, 128), BF16)

    @pl.when(s == ns - 1)
    def _():
        fx[3] = jnp.zeros((3, 576, 128), BF16)

    for r in range(2):
        for b in range(9):
            window[r, :, 128 * b : 128 * b + 128] = fx[r + b // 3, b % 3]

    def gather_step(step, carry):
        gather(step, codes, window, got)
        return carry

    lax.fori_loop(0, 24, gather_step, 0)

    def aggregate_step(step, carry):
        aggregate(step, geo, wgt, got, agg)
        return carry

    lax.fori_loop(0, 2 * (64 // TILE), aggregate_step, 0)
    readout(agg, read3[...], read_t3[...], out_col[...], energies)

    def backward_step(step, carry):
        backward(step, geo, wgt, got, agg, slopes)
        return carry

    lax.fori_loop(0, 48, backward_step, 0)
    forces[...] = jnp.zeros_like(forces)
    for r in range(2):
        centre = edge_forces(r, geo, unit, slopes, edge)
        scatter(r, codes, edge, lhs, hot, centre, forces)

    for i, (ds, dt) in enumerate(BACK):
        src = forces.at[1 + dt, pl.ds(2 if ds == 0 else 0, 2)]
        flights[TAIL + i] = copy(TAIL + i, src, tail.at[i], at(ds, dt))
        flights[TAIL + i].start()
    for i in range(5):
        flights[TAIL + i].wait_recv()
    front = s == ns - 1
    above = tail[2] + tail[3] + tail[4]
    force = forces[1, 2:4] + tail[0] + tail[1] + jnp.where(front, 0.0, above)
    force = force[:, 0:3]
    vel = velocities[1, 0] + KICK_FACTOR * force[0]
    new_vel[0, 0] = vel
    new_pos[0, 0] = positions[1, 0] + MOVE_FACTOR * vel
    vel = vel_in[...] + KICK_FACTOR * force[1]
    new_vel[1, 0] = jnp.where(front, fresh_vel[0], vel)
    new_pos[1, 0] = jnp.where(front, fresh_pos[0], pos[3, 1] + MOVE_FACTOR * vel)
    for i in range(5):
        flights[TAIL + i].wait_send()


def local(
    positions, velocities, features, neighbours, counts, w_first, w_second, w_read, w_out,
    fresh_positions, fresh_velocities,
):
    vmem = pl.BlockSpec(memory_space=pltpu.VMEM)
    whole = pl.BlockSpec(memory_space=pl.ANY)
    return pl.pallas_call(
        step_kernel,
        out_shape=(
            jax.ShapeDtypeStruct((2, 1, 128), F32),
            jax.ShapeDtypeStruct((2, 1, 3, 128), F32),
            jax.ShapeDtypeStruct((2, 1, 3, 128), F32),
        ),
        in_specs=[vmem, vmem, whole] + [vmem] * 8,
        out_specs=(vmem, vmem, vmem),
        scratch_shapes=[
            pltpu.VMEM((4, 3, 3, 128), F32),
            pltpu.VMEM((3, 128), F32),
            pltpu.VMEM((4, 3, 576, 128), BF16),
            pltpu.VMEM((2, GEO, 24, 128), F32),
            pltpu.VMEM((2, 3, 24, 128), F32),
            pltpu.VMEM((32, 256 * SPAN), BF16),
            pltpu.VMEM((192, 256 * SPAN), BF16),
            pltpu.VMEM((2, 24, 2, 192, 128), F32),
            pltpu.VMEM((2, 576, 1152), BF16),
            pltpu.VMEM((2, 24, 576, 128), F32),
            pltpu.VMEM((2, 9, 64, 128), F32),
            pltpu.VMEM((2, 9, 24, 128), F32),
            pltpu.VMEM((3, 24, 128), F32),
            pltpu.VMEM((80, 3072), BF16),
            pltpu.VMEM((128, 3072), BF16),
            pltpu.VMEM((3, 4, 8, 128), F32),
            pltpu.VMEM((5, 2, 8, 128), F32),
            pltpu.VMEM((64, 32), BF16),
            pltpu.VMEM((192, 192), BF16),
            pltpu.VMEM((128, 576), BF16),
            pltpu.VMEM((384, 192), BF16),
            pltpu.VMEM((128, 256), F32),
            pltpu.SemaphoreType.DMA,
            pltpu.SemaphoreType.DMA((COPIES,)),
            pltpu.SemaphoreType.DMA((COPIES,)),
        ],
        compiler_params=pltpu.CompilerParams(
            vmem_limit_bytes=56 << 20, collective_id=0, has_side_effects=True
        ),
        name="step",
    )(
        positions, velocities, features, neighbours, counts, w_first, w_second, w_read,
        w_out[None], fresh_positions, fresh_velocities,
    )


def solution(mesh):
    spec = P("shock", "trans", None, None)
    return jax.shard_map(
        local,
        mesh=mesh,
        in_specs=(
            spec, spec, spec, spec, P("shock", "trans", None), P(), P(), P(), P(),
            P("trans", None, None), P("trans", None, None),
        ),
        out_specs=(P("shock", "trans", None), spec, spec),
        check_vma=False,
    )
```

```python
import math

import jax
import jax.numpy as jnp
from jax import lax
from jax.experimental import pallas as pl
from jax.experimental.pallas import tpu as pltpu
from jax.sharding import PartitionSpec as P

CUTOFF_RADIUS = 9.5
BLOCK_LENGTH = 13.2
KICK_FACTOR = 4.0
MOVE_FACTOR = 0.5
F32 = jnp.float32
BF16 = jnp.bfloat16
GEO = 12
SPAN = 24


def split(x):
    hi = x.astype(BF16)
    return hi, (x - hi.astype(F32)).astype(BF16)


def sigmoid(z):
    return 0.5 * jnp.tanh(0.5 * z) + 0.5


def sin_cos_pi(t):
    whole = jnp.floor(t + 0.5)
    half = whole * 0.5
    sign = 1.0 - 4.0 * (half - jnp.floor(half))
    r = (t - whole) * math.pi
    r2 = r * r
    s = r * (1.0 + r2 * (-1 / 6 + r2 * (1 / 120 + r2 * (-1 / 5040 + r2 * (1 / 362880 - r2 / 39916800)))))
    c = 1.0 + r2 * (
        -1 / 2 + r2 * (1 / 24 + r2 * (-1 / 720 + r2 * (1 / 40320 + r2 * (-1 / 3628800 + r2 / 479001600))))
    )
    return s * sign, c * sign


def block_at(r, kk):
    if kk < 2:
        return 1 + kk, 0
    if kk == 2:
        return 3 * r, 0
    return r + (kk - 3) % 3, (kk - 3) // 3 + 1


def places(r, way, codes, place):
    code = codes[r, 0]
    cell = code >> 7
    iz = (cell >= 9).astype(jnp.int32) + (cell >= 18).astype(jnp.int32)
    k = cell - 9 * iz
    is_ = (k >= 3).astype(jnp.int32) + (k >= 6).astype(jnp.int32)
    it = k - 3 * is_ - 1
    centre = jnp.where(is_ == 0, 2, is_ - 1) if r == 0 else is_
    kk = jnp.where(it == 0, centre, jnp.where(it == way, 3, 6) + is_)
    place[r] = kk * 128 + (code & 127)


def geometry(r, pos, codes, place, counts, geo, unit):
    for part in range(3):
        rows = slice(8 * part, 8 * part + 8)
        code = codes[r, 0, rows, :]
        j = code & 127
        cell = code >> 7
        iz = (cell >= 9).astype(jnp.int32) + (cell >= 18).astype(jnp.int32)
        k = cell - 9 * iz
        is_ = (k >= 3).astype(jnp.int32) + (k >= 6).astype(jnp.int32)
        it = k - 3 * is_
        kk = place[r, rows, :] >> 7
        shifts = [(v - 1).astype(F32) * BLOCK_LENGTH for v in (is_, it, iz)]
        delta = []
        for comp in range(3):
            other = jnp.zeros((8, 128), F32)
            for b in range(9):
                row, role = block_at(r, b)
                row = pos[row, role, comp, pl.ds(0, 8, stride=0), :]
                got = jnp.take_along_axis(row, j, axis=1, mode="promise_in_bounds")
                other = jnp.where(kk == b, got, other)
            centre = pos[r + 1, 0, comp, pl.ds(0, 8, stride=0), :]
            delta.append(other + shifts[comp] - centre)
        dx, dy, dz = delta
        d = jnp.sqrt(dx * dx + dy * dy + dz * dz)
        rinv = 1.0 / d
        ux, uy, uz = dx * rinv, dy * rinv, dz * rinv
        x = d * (1.0 / CUTOFF_RADIUS)
        x2 = x * x
        x4 = x2 * x2
        slot = lax.broadcasted_iota(jnp.int32, (8, 128), 0) + 8 * part
        live = jnp.where(slot < counts[r, pl.ds(0, 8, stride=0), :], 1.0 / 24.0, 0.0)
        env = (1.0 + x4 * x2 * (-28.0 + x * (48.0 - 21.0 * x))) * live
        slope = (-168.0 / CUTOFF_RADIUS) * x4 * x * ((1.0 - x) * (1.0 - x)) * live
        r3, r5, r15 = math.sqrt(3.0), math.sqrt(5.0), math.sqrt(15.0)
        values = [
            r3 * ux,
            r3 * uy,
            r3 * uz,
            r15 * ux * uy,
            r15 * uy * uz,
            0.5 * r5 * (3.0 * uz * uz - 1.0),
            r15 * ux * uz,
            0.5 * r15 * (ux * ux - uy * uy),
            x,
            rinv,
            env,
            slope,
        ]
        for q, v in enumerate(values):
            geo[r, q, rows, :] = v
        for q, v in enumerate((ux, uy, uz)):
            unit[r, q, rows, :] = v


def radial(step, geo, first, second, basis, hid, wgt):
    per = 24 // SPAN
    r = step // per
    n0 = (step % per) * SPAN
    order = (lax.broadcasted_iota(jnp.int32, (8, 128), 0) + 1).astype(F32)
    scale = math.sqrt(2.0 / CUTOFF_RADIUS)
    zero8 = jnp.zeros((8, 128), F32)
    for q in range(SPAN):
        x = geo[r, 8, pl.ds(n0 + q, 8, stride=0), :]
        rinv = geo[r, 9, pl.ds(n0 + q, 8, stride=0), :]
        s, c = sin_cos_pi(x * order)
        b = (scale * rinv) * s
        bd = rinv * ((scale * math.pi / CUTOFF_RADIUS) * order * c - b)
        for v, at in ((b, q), (bd, SPAN + q)):
            hi = v.astype(BF16).astype(F32)
            lanes = slice(128 * at, 128 * at + 128)
            basis[0:16, lanes] = jnp.concatenate([hi, v - hi], axis=0).astype(BF16)
            basis[16:32, lanes] = jnp.concatenate([hi, zero8], axis=0).astype(BF16)
    z = jnp.dot(first, basis[...], preferred_element_type=F32)
    for q in range(SPAN):
        env = geo[r, 10, pl.ds(n0 + q, 8, stride=0), :]
        slope = geo[r, 11, pl.ds(n0 + q, 8, stride=0), :]
        env, slope = (jnp.concatenate([v] * 8, axis=0) for v in (env, slope))
        zq = z[:, 128 * q : 128 * q + 128]
        zd = z[:, 128 * (SPAN + q) : 128 * (SPAN + q) + 128]
        sig = sigmoid(zq)
        act = zq * sig
        h = act * env
        hd = (sig + act * (1.0 - sig)) * zd * env + act * slope
        for v, at in ((h, q), (hd, SPAN + q)):
            hi, lo = split(v)
            lanes = slice(128 * at, 128 * at + 128)
            hid[0:64, lanes] = hi
            hid[64:128, lanes] = lo
            hid[128:192, lanes] = hi
    w = jnp.dot(second, hid[...], preferred_element_type=F32)
    for q in range(SPAN):
        wgt[r, n0 + q, 0] = w[:, 128 * q : 128 * q + 128]
        wgt[r, n0 + q, 1] = w[:, 128 * (SPAN + q) : 128 * (SPAN + q) + 128]


STAGES = ((0, 2), (2, 6), (6, 9))


def gather(r, stage, step, place, fx, got):
    n0 = step * 2
    first, last = STAGES[stage]
    ids = lax.broadcasted_iota(jnp.int32, (128, 128), 0).astype(F32).astype(BF16)
    halves = []
    for q in range(2):
        at = place[r, pl.ds(n0 + q, 16, stride=0), :]
        j = (at & 127).astype(F32)
        kk = at >> 7
        pieces = []
        for b in range(first, last):
            val = jnp.where(kk == b, j, -1.0).astype(BF16)
            val = jnp.concatenate([val] * 8, axis=0)
            pieces.append(jnp.where(val == ids, jnp.ones((), BF16), jnp.zeros((), BF16)))
        halves.append(jnp.concatenate(pieces, axis=0))
    hot = jnp.concatenate(halves, axis=1)
    rows = [fx[block_at(r, b)] for b in range(first, last)]
    out = jnp.dot(jnp.concatenate(rows, axis=1), hot, preferred_element_type=F32)
    for q in range(2):
        part = out[:, 128 * q : 128 * q + 128]
        got[r, n0 + q] = part if stage == 0 else got[r, n0 + q] + part


def hot_rows(r, place, hot_t):
    j = (place[r] & 127).astype(F32)
    cols = jnp.concatenate([j, jnp.zeros((104, 128), F32)], axis=0).T
    ids = lax.broadcasted_iota(jnp.int32, (128, 128), 1).astype(F32)
    for n in range(24):
        same = jnp.broadcast_to(cols[:, n : n + 1], (128, 128)) == ids
        hot_t[r, 128 * n : 128 * n + 128, :] = jnp.where(same, 1.0, 0.0).astype(BF16)


def row8(ref, r, q, n, times=1):
    v = ref[r, q, pl.ds(n, 8, stride=0), :]
    return v if times == 1 else jnp.concatenate([v] * times, axis=0)


TILE = 16


def aggregate(step, geo, wgt, got, agg):
    per = 64 // TILE
    r = step // per
    c0 = pl.multiple_of((step % per) * TILE, TILE)

    def body(n, acc):
        acc = list(acc)
        y = [None] + [row8(geo, r, q, n, TILE // 8) for q in range(8)]
        x = [got[r, n, pl.ds(m * 64 + c0, TILE), :] for m in range(9)]
        w = [wgt[r, n, 0, pl.ds(p * 64 + c0, TILE), :] for p in range(3)]
        p0 = w[0] * x[0]
        v = x[1] * y[1] + x[2] * y[2] + x[3] * y[3]
        acc[0] += p0 + w[1] * x[0] + w[2] * v
        for m in range(1, 9):
            acc[m] += p0 * y[m] + w[1] * x[m]
        return tuple(acc)

    acc = lax.fori_loop(0, 24, body, (jnp.zeros((TILE, 128), F32),) * 9, unroll=8)
    for m in range(9):
        agg[r, m, pl.ds(c0, TILE), :] = acc[m]


def readout(agg, read3, read_t3, w_out, energies):
    inv = []
    for r in range(2):
        a = [agg[r, m] for m in range(9)]
        sq = [v * v for v in a]
        inv.append(
            jnp.concatenate(
                [sq[0], sq[1] + sq[2] + sq[3], sq[4] + sq[5] + sq[6] + sq[7] + sq[8]], axis=0
            )
        )
    s = jnp.concatenate(inv, axis=1)
    hi, lo = split(s)
    z = jnp.dot(read3, jnp.concatenate([hi, lo, hi], axis=0), preferred_element_type=F32)
    sig = sigmoid(z)
    act = z * sig
    energy = jnp.sum(w_out * act, axis=0, keepdims=True)
    energies[0] = energy[:, :128]
    energies[1] = energy[:, 128:]
    gz = w_out * (sig + act * (1.0 - sig))
    hi, lo = split(gz)
    gs = jnp.dot(read_t3, jnp.concatenate([hi, lo, hi], axis=0), preferred_element_type=F32)
    gs = gs + gs
    for r in range(2):
        g = gs[:, 128 * r : 128 * r + 128]
        for m in range(9):
            part = 0 if m == 0 else 1 if m < 4 else 2
            agg[r, m] = agg[r, m] * g[64 * part : 64 * part + 64]


def backward(step, geo, wgt, got, agg, slopes):
    r = step // 24
    n = step % 24
    y = [None] + [row8(geo, r, q, n) for q in range(8)]
    acc = [jnp.zeros((8, 128), F32)] * 9
    for c in range(8):
        x = [got[r, n, m * 64 + 8 * c : m * 64 + 8 * c + 8, :] for m in range(9)]
        g = [agg[r, m, 8 * c : 8 * c + 8, :] for m in range(9)]
        w0, _, w2 = [wgt[r, n, 0, p * 64 + 8 * c : p * 64 + 8 * c + 8, :] for p in range(3)]
        d0, d1, d2 = [wgt[r, n, 1, p * 64 + 8 * c : p * 64 + 8 * c + 8, :] for p in range(3)]
        gx = g[0] * x[0]
        gy = g[0]
        for m in range(1, 9):
            gx += g[m] * x[m]
            gy += g[m] * y[m]
        v = x[1] * y[1] + x[2] * y[2] + x[3] * y[3]
        acc[0] += d1 * gx + d0 * (gy * x[0]) + d2 * (g[0] * v)
        p0 = w0 * x[0]
        p2 = w2 * g[0]
        for m in range(1, 9):
            acc[m] += p0 * g[m] + p2 * x[m] if m < 4 else p0 * g[m]
    for q in range(9):
        slopes[r, q, pl.ds(n, 1), :] = jnp.sum(acc[q], axis=0, keepdims=True)


def edge_forces(r, geo, unit, slopes, edge):
    r3, r5, r15 = math.sqrt(3.0), math.sqrt(5.0), math.sqrt(15.0)
    ux, uy, uz = (unit[r, q] for q in range(3))
    rinv = geo[r, 9]
    gd, g1, g2, g3, g4, g5, g6, g7, g8 = (slopes[r, q] for q in range(9))
    gx = r3 * g1 + r15 * (uy * g4 + uz * g7 + ux * g8)
    gy = r3 * g2 + r15 * (ux * g4 + uz * g5 - uy * g8)
    gz = r3 * g3 + r15 * (uy * g5 + ux * g7) + (3.0 * r5) * uz * g6
    along = gd - (gx * ux + gy * uy + gz * uz) * rinv
    out = []
    for q, (g, u) in enumerate(((gx, ux), (gy, uy), (gz, uz))):
        f = g * rinv + along * u
        edge[q] = f
        out.append(jnp.sum(f, axis=0, keepdims=True))
    return out


def scatter(r, place, edge, lhs, hot_t, centre, forces):
    pick = lax.broadcasted_iota(jnp.int32, (8, 128), 0)

    def body(n, carry):
        kk = place[r, pl.ds(n, 8, stride=0), :] >> 7
        value = jnp.zeros((8, 128), F32)
        for q in range(3):
            f = edge[q, pl.ds(n, 8, stride=0), :]
            hi = f.astype(BF16).astype(F32)
            value = jnp.where(pick == q, hi, jnp.where(pick == q + 3, f - hi, value))
        rows = [jnp.where(kk == b, value, 0.0) for b in range(9)] + [jnp.zeros((8, 128), F32)]
        lanes = pl.ds(pl.multiple_of(n * 128, 128), 128)
        lhs[:, lanes] = jnp.concatenate(rows, axis=0).astype(BF16)
        return carry

    lax.fori_loop(0, 24, body, 0, unroll=4)
    out = jnp.dot(lhs[...], hot_t[r], preferred_element_type=F32)
    for b in range(9):
        row, role = block_at(r, b)
        for q in range(3):
            v = -(out[8 * b + q : 8 * b + q + 1] + out[8 * b + q + 3 : 8 * b + q + 4])
            if row == r + 1 and role == 0:
                v += centre[q]
            forces[role, row, q] += v


def stack(w, axis):
    hi, lo = split(w)
    return jnp.concatenate([hi, hi, lo], axis=axis)


POS = 0
VEL = 8
OWN = 9
CHIP = 11
OFF = 12
CORNER = 13
FAR = 14
NEAR_CHIP = 16
FAR_CHIP = 17
FAR_CORNER = 18
TAIL = 19
COPIES = 24
AROUND = ((-1, -1), (-1, 0), (-1, 1), (0, -1), (0, 1), (1, -1), (1, 0), (1, 1))
BACK = ((0, 1), (0, -1), (-1, 1), (-1, 0), (-1, -1))


def step_kernel(
    positions_in, velocities_in, features, codes_in, counts_in, w_first_in, w_second_in, w_read_in,
    w_out_in, fresh_pos_in, fresh_vel_in, energies, new_pos, new_vel,
    positions, velocities, codes, counts, w_first, w_second, w_read, w_out, fresh_pos, fresh_vel,
    pos, vel_in, fx, place, geo, unit, basis, hid, wgt, got, agg, slopes, edge, lhs, hot_t,
    forces, tail, first, second, read3, read_t3, out_col, own_sem, load_sem, send_sem, recv_sem,
):
    s = lax.axis_index("shock")
    t = lax.axis_index("trans")
    ns = lax.axis_size("shock")
    nt = lax.axis_size("trans")
    core = lax.rem(s, 2)
    way = 1 - 2 * lax.rem(t, 2)
    out_way = 2 * core - 1

    def at(ds, dt):
        return (lax.rem(s + ds + ns, ns), lax.rem(t + dt + nt, nt))

    def copy(k, src, dst, to):
        return pltpu.make_async_remote_copy(
            src_ref=src,
            dst_ref=dst,
            send_sem=send_sem.at[k],
            recv_sem=recv_sem.at[k],
            device_id=to,
            device_id_type=pl.DeviceIdType.MESH,
        )

    barrier = pltpu.get_barrier_semaphore()
    for ds, dt in AROUND + ((0, 2), (0, -2)):
        pl.semaphore_signal(
            barrier, inc=1, device_id=at(ds, dt), device_id_type=pl.DeviceIdType.MESH
        )
    own = pltpu.make_async_copy(features.at[:, 0], fx.at[pl.ds(1, 2), 0], own_sem)
    loads = [
        pltpu.make_async_copy(src, dst, load_sem.at[i])
        for i, (src, dst) in enumerate(
            (
                (codes_in, codes),
                (positions_in, positions),
                (counts_in, counts),
                (w_first_in, w_first),
                (w_second_in, w_second),
                (w_read_in, w_read),
                (w_out_in, w_out),
                (velocities_in, velocities),
                (fresh_pos_in, fresh_pos),
                (fresh_vel_in, fresh_vel),
                (positions_in, pos.at[pl.ds(1, 2), 0]),
            )
        )
    ]
    own.start()
    for load in loads:
        load.start()
    loads[0].wait()
    for r in range(2):
        places(r, way, codes, place)
    pl.semaphore_wait(barrier, 10)

    flights = {}

    def role(dt):
        return 0 if dt == 0 else (3 - dt * way) // 2

    for i, (ds, dt) in enumerate(AROUND):
        if ds == 0:
            src, dst = positions_in, pos.at[pl.ds(1, 2), role(dt)]
        elif ds == 1:
            src, dst = positions_in.at[1], pos.at[0, role(dt)]
        else:
            src, dst = positions_in.at[0], pos.at[3, role(dt)]
        flights[POS + i] = copy(POS + i, src, dst, at(ds, dt))
    flights[VEL] = copy(VEL, velocities_in.at[0], vel_in, at(-1, 0))
    chip_row, chip_ghost = 1 - core, 3 * core
    off_row, off_ghost = core, 3 * (1 - core)
    order = (chip_row, off_row)
    for i in range(2):
        flights[OWN + i] = copy(OWN + i, features.at[order[i], 0], fx.at[1 + order[i], 1], at(0, way))
    flights[CHIP] = copy(CHIP, features.at[chip_row, 0], fx.at[chip_ghost, 0], at(-out_way, 0))
    flights[OFF] = copy(OFF, features.at[off_row, 0], fx.at[off_ghost, 0], at(out_way, 0))
    flights[CORNER] = copy(CORNER, features.at[off_row, 0], fx.at[off_ghost, 1], at(out_way, way))
    for k in list(range(POS, POS + 8)) + [OWN, OWN + 1, CORNER, OFF, CHIP, VEL]:
        flights[k].start()
    my_off_ghost = 3 * core
    for i in range(2):
        row = 1 + order[i]
        flights[FAR + i] = copy(FAR + i, fx.at[row, 1], fx.at[row, 2], at(0, 2 * way))
    flights[FAR_CORNER] = copy(
        FAR_CORNER, fx.at[my_off_ghost, 1], fx.at[my_off_ghost, 2], at(0, 2 * way)
    )
    flights[NEAR_CHIP] = copy(
        NEAR_CHIP, fx.at[1 + chip_row, 1], fx.at[chip_ghost, 1], at(-out_way, 0)
    )
    flights[FAR_CHIP] = copy(
        FAR_CHIP, fx.at[1 + chip_row, 2], fx.at[chip_ghost, 2], at(-out_way, 0)
    )

    def gather_stage(r, stage):
        def gather_step(step, carry):
            gather(r, stage, step, place, fx, got)
            return carry

        lax.fori_loop(0, 12, gather_step, 0, unroll=4)

    own.wait()
    for r in range(2):
        gather_stage(r, 0)

    for load in loads[1:]:
        load.wait()
    first[...] = jnp.concatenate([stack(w_first[...].T, 1), jnp.zeros((64, 8), BF16)], axis=1)
    second[...] = stack(w_second[...].T, 1)
    read3[...] = stack(w_read[...].T, 1)
    read_t3[...] = stack(w_read[...], 1)
    col = jnp.broadcast_to(w_out[...], (128, 128)).T
    out_col[...] = jnp.concatenate([col, col], axis=1)
    flights[OWN].wait_recv()
    flights[FAR].start()
    flights[NEAR_CHIP].start()
    for r in range(2):
        hot_rows(r, place, hot_t)

    for k in range(POS, POS + 8):
        flights[k].wait_recv()

    @pl.when(s == 0)
    def _():
        pos[0] = jnp.zeros((3, 3, 1, 128), F32)

    @pl.when(s == ns - 1)
    def _():
        pos[3] = jnp.zeros((3, 3, 1, 128), F32)

    for r in range(2):
        geometry(r, pos, codes, place, counts, geo, unit)

    def radial_steps(lo, hi):
        def radial_step(step, carry):
            radial(step, geo, first[...], second[...], basis, hid, wgt)
            return carry

        lax.fori_loop(lo, hi, radial_step, 0)

    total = 48 // SPAN
    radial_steps(0, total // 2)
    flights[OWN + 1].wait_recv()
    flights[FAR + 1].start()
    radial_steps(total // 2, total)
    flights[FAR].wait_recv()
    flights[FAR_CHIP].start()
    flights[CORNER].wait_recv()
    flights[FAR_CORNER].start()
    for k in (CHIP, OFF, NEAR_CHIP):
        flights[k].wait_recv()
    flights[FAR_CORNER].wait_send()
    blank = jnp.zeros((576, 128), BF16)

    def close(role):
        @pl.when(s == 0)
        def _():
            fx[0, role] = blank

        @pl.when(s == ns - 1)
        def _():
            fx[3, role] = blank

    close(0)
    close(1)
    gather_stage(0, 1)
    gather_stage(1, 1)
    for k in (FAR + 1, FAR_CORNER, FAR_CHIP):
        flights[k].wait_recv()
    close(2)
    for r in range(2):
        gather_stage(r, 2)

    def aggregate_step(step, carry):
        aggregate(step, geo, wgt, got, agg)
        return carry

    lax.fori_loop(0, 2 * (64 // TILE), aggregate_step, 0)
    readout(agg, read3[...], read_t3[...], out_col[...], energies)

    def backward_step(step, carry):
        backward(step, geo, wgt, got, agg, slopes)
        return carry

    lax.fori_loop(0, 48, backward_step, 0, unroll=2)
    forces[...] = jnp.zeros_like(forces)
    for r in range(2):
        centre = edge_forces(r, geo, unit, slopes, edge)
        scatter(r, place, edge, lhs, hot_t, centre, forces)

    for i, (ds, dt) in enumerate(BACK):
        src = forces.at[role(dt), pl.ds(2 if ds == 0 else 0, 2)]
        flights[TAIL + i] = copy(TAIL + i, src, tail.at[i], at(ds, dt))
        flights[TAIL + i].start()
    for k in list(range(FAR_CORNER)):
        flights[k].wait_send()
    flights[VEL].wait_recv()
    for i in range(5):
        flights[TAIL + i].wait_recv()
    front = s == ns - 1
    above = tail[2] + tail[3] + tail[4]
    force = forces[0, 2:4] + tail[0] + tail[1] + jnp.where(front, 0.0, above)
    vel = velocities[1] + KICK_FACTOR * force[0]
    new_vel[0] = vel
    new_pos[0] = positions[1] + MOVE_FACTOR * vel
    vel = vel_in[...] + KICK_FACTOR * force[1]
    new_vel[1] = jnp.where(front, fresh_vel[...], vel)
    new_pos[1] = jnp.where(front, fresh_pos[...], pos[3, 0] + MOVE_FACTOR * vel)
    for i in range(5):
        flights[TAIL + i].wait_send()


def local(
    positions, velocities, features, neighbours, counts, w_first, w_second, w_read, w_out,
    fresh_positions, fresh_velocities,
):
    vmem = pl.BlockSpec(memory_space=pltpu.VMEM)
    whole = pl.BlockSpec(memory_space=pl.ANY)
    energies, new_pos, new_vel = pl.pallas_call(
        step_kernel,
        out_shape=(
            jax.ShapeDtypeStruct((2, 1, 128), F32),
            jax.ShapeDtypeStruct((2, 3, 1, 128), F32),
            jax.ShapeDtypeStruct((2, 3, 1, 128), F32),
        ),
        in_specs=[whole] * 11,
        out_specs=(vmem, vmem, vmem),
        scratch_shapes=[
            pltpu.VMEM((2, 3, 1, 128), F32),
            pltpu.VMEM((2, 3, 1, 128), F32),
            pltpu.VMEM((2, 1, 24, 128), jnp.int32),
            pltpu.VMEM((2, 1, 128), jnp.int32),
            pltpu.VMEM((8, 64), F32),
            pltpu.VMEM((64, 192), F32),
            pltpu.VMEM((192, 128), F32),
            pltpu.VMEM((1, 128), F32),
            pltpu.VMEM((3, 1, 128), F32),
            pltpu.VMEM((3, 1, 128), F32),
            pltpu.VMEM((4, 3, 3, 1, 128), F32),
            pltpu.VMEM((3, 1, 128), F32),
            pltpu.VMEM((4, 3, 576, 128), BF16),
            pltpu.VMEM((2, 24, 128), jnp.int32),
            pltpu.VMEM((2, GEO, 24, 128), F32),
            pltpu.VMEM((2, 3, 24, 128), F32),
            pltpu.VMEM((32, 256 * SPAN), BF16),
            pltpu.VMEM((192, 256 * SPAN), BF16),
            pltpu.VMEM((2, 24, 2, 192, 128), F32),
            pltpu.VMEM((2, 24, 576, 128), F32),
            pltpu.VMEM((2, 9, 64, 128), F32),
            pltpu.VMEM((2, 9, 24, 128), F32),
            pltpu.VMEM((3, 24, 128), F32),
            pltpu.VMEM((80, 3072), BF16),
            pltpu.VMEM((2, 3072, 128), BF16),
            pltpu.VMEM((3, 4, 3, 1, 128), F32),
            pltpu.VMEM((5, 2, 3, 1, 128), F32),
            pltpu.VMEM((64, 32), BF16),
            pltpu.VMEM((192, 192), BF16),
            pltpu.VMEM((128, 576), BF16),
            pltpu.VMEM((192, 384), BF16),
            pltpu.VMEM((128, 256), F32),
            pltpu.SemaphoreType.DMA,
            pltpu.SemaphoreType.DMA((11,)),
            pltpu.SemaphoreType.DMA((COPIES,)),
            pltpu.SemaphoreType.DMA((COPIES,)),
        ],
        compiler_params=pltpu.CompilerParams(
            vmem_limit_bytes=56 << 20, collective_id=0, has_side_effects=True
        ),
        name="step",
    )(
        positions.transpose(0, 2, 1, 3), velocities.transpose(0, 2, 1, 3), features, neighbours,
        counts, w_first.T, w_second.T, w_read.T, w_out[None],
        fresh_positions.transpose(1, 0, 2), fresh_velocities.transpose(1, 0, 2),
    )
    return energies, new_pos.transpose(0, 2, 1, 3), new_vel.transpose(0, 2, 1, 3)


def solution(mesh):
    spec = P("shock", "trans", None, None)
    return jax.shard_map(
        local,
        mesh=mesh,
        in_specs=(
            spec, spec, spec, spec, P("shock", "trans", None), P(), P(), P(), P(),
            P("trans", None, None), P("trans", None, None),
        ),
        out_specs=(P("shock", "trans", None), spec, spec),
        check_vma=False,
    )
```

```python
import math

import jax
import jax.numpy as jnp
from jax import lax
from jax.experimental import pallas as pl
from jax.experimental.pallas import tpu as pltpu
from jax.sharding import PartitionSpec as P

CUTOFF_RADIUS = 9.5
BLOCK_LENGTH = 13.2
KICK_FACTOR = 4.0
MOVE_FACTOR = 0.5
F32 = jnp.float32
BF16 = jnp.bfloat16
GEO = 12
SPAN = 24


def split(x):
    hi = x.astype(BF16)
    return hi, (x - hi.astype(F32)).astype(BF16)


def sigmoid(z):
    return 0.5 * jnp.tanh(0.5 * z) + 0.5


def sin_cos_pi(t):
    whole = jnp.floor(t + 0.5)
    half = whole * 0.5
    sign = 1.0 - 4.0 * (half - jnp.floor(half))
    r = (t - whole) * math.pi
    r2 = r * r
    s = r * (1.0 + r2 * (-1 / 6 + r2 * (1 / 120 + r2 * (-1 / 5040 + r2 * (1 / 362880 - r2 / 39916800)))))
    c = 1.0 + r2 * (
        -1 / 2 + r2 * (1 / 24 + r2 * (-1 / 720 + r2 * (1 / 40320 + r2 * (-1 / 3628800 + r2 / 479001600))))
    )
    return s * sign, c * sign


def block_at(r, kk):
    if kk < 2:
        return 1 + kk, 0
    if kk == 2:
        return 3 * r, 0
    return r + (kk - 3) % 3, (kk - 3) // 3 + 1


def places(r, way, codes, place):
    code = codes[r, 0]
    cell = code >> 7
    iz = (cell >= 9).astype(jnp.int32) + (cell >= 18).astype(jnp.int32)
    k = cell - 9 * iz
    is_ = (k >= 3).astype(jnp.int32) + (k >= 6).astype(jnp.int32)
    it = k - 3 * is_ - 1
    centre = jnp.where(is_ == 0, 2, is_ - 1) if r == 0 else is_
    kk = jnp.where(it == 0, centre, jnp.where(it == way, 3, 6) + is_)
    place[r] = kk * 128 + (code & 127)


def geometry(r, pos, codes, place, counts, geo, unit):
    for part in range(3):
        rows = slice(8 * part, 8 * part + 8)
        code = codes[r, 0, rows, :]
        j = code & 127
        cell = code >> 7
        iz = (cell >= 9).astype(jnp.int32) + (cell >= 18).astype(jnp.int32)
        k = cell - 9 * iz
        is_ = (k >= 3).astype(jnp.int32) + (k >= 6).astype(jnp.int32)
        it = k - 3 * is_
        kk = place[r, rows, :] >> 7
        shifts = [(v - 1).astype(F32) * BLOCK_LENGTH for v in (is_, it, iz)]
        delta = []
        for comp in range(3):
            other = jnp.zeros((8, 128), F32)
            for b in range(9):
                row, role = block_at(r, b)
                row = pos[row, role, comp, pl.ds(0, 8, stride=0), :]
                got = jnp.take_along_axis(row, j, axis=1, mode="promise_in_bounds")
                other = jnp.where(kk == b, got, other)
            centre = pos[r + 1, 0, comp, pl.ds(0, 8, stride=0), :]
            delta.append(other + shifts[comp] - centre)
        dx, dy, dz = delta
        d = jnp.sqrt(dx * dx + dy * dy + dz * dz)
        rinv = 1.0 / d
        ux, uy, uz = dx * rinv, dy * rinv, dz * rinv
        x = d * (1.0 / CUTOFF_RADIUS)
        x2 = x * x
        x4 = x2 * x2
        slot = lax.broadcasted_iota(jnp.int32, (8, 128), 0) + 8 * part
        live = jnp.where(slot < counts[r, pl.ds(0, 8, stride=0), :], 1.0 / 24.0, 0.0)
        env = (1.0 + x4 * x2 * (-28.0 + x * (48.0 - 21.0 * x))) * live
        slope = (-168.0 / CUTOFF_RADIUS) * x4 * x * ((1.0 - x) * (1.0 - x)) * live
        r3, r5, r15 = math.sqrt(3.0), math.sqrt(5.0), math.sqrt(15.0)
        values = [
            r3 * ux,
            r3 * uy,
            r3 * uz,
            r15 * ux * uy,
            r15 * uy * uz,
            0.5 * r5 * (3.0 * uz * uz - 1.0),
            r15 * ux * uz,
            0.5 * r15 * (ux * ux - uy * uy),
            x,
            rinv,
            env,
            slope,
        ]
        for q, v in enumerate(values):
            geo[r, q, rows, :] = v
        for q, v in enumerate((ux, uy, uz)):
            unit[r, q, rows, :] = v


def radial(step, geo, first, second, basis, hid, wgt):
    per = 24 // SPAN
    r = step // per
    n0 = (step % per) * SPAN
    order = (lax.broadcasted_iota(jnp.int32, (8, 128), 0) + 1).astype(F32)
    scale = math.sqrt(2.0 / CUTOFF_RADIUS)
    zero8 = jnp.zeros((8, 128), F32)
    for q in range(SPAN):
        x = geo[r, 8, pl.ds(n0 + q, 8, stride=0), :]
        rinv = geo[r, 9, pl.ds(n0 + q, 8, stride=0), :]
        s, c = sin_cos_pi(x * order)
        b = (scale * rinv) * s
        bd = rinv * ((scale * math.pi / CUTOFF_RADIUS) * order * c - b)
        for v, at in ((b, q), (bd, SPAN + q)):
            hi = v.astype(BF16).astype(F32)
            lanes = slice(128 * at, 128 * at + 128)
            basis[0:16, lanes] = jnp.concatenate([hi, v - hi], axis=0).astype(BF16)
            basis[16:32, lanes] = jnp.concatenate([hi, zero8], axis=0).astype(BF16)
    z = jnp.dot(first, basis[...], preferred_element_type=F32)
    for q in range(SPAN):
        env = geo[r, 10, pl.ds(n0 + q, 8, stride=0), :]
        slope = geo[r, 11, pl.ds(n0 + q, 8, stride=0), :]
        env, slope = (jnp.concatenate([v] * 8, axis=0) for v in (env, slope))
        zq = z[:, 128 * q : 128 * q + 128]
        zd = z[:, 128 * (SPAN + q) : 128 * (SPAN + q) + 128]
        sig = sigmoid(zq)
        act = zq * sig
        h = act * env
        hd = (sig + act * (1.0 - sig)) * zd * env + act * slope
        for v, at in ((h, q), (hd, SPAN + q)):
            hi, lo = split(v)
            lanes = slice(128 * at, 128 * at + 128)
            hid[0:64, lanes] = hi
            hid[64:128, lanes] = lo
            hid[128:192, lanes] = hi
    w = jnp.dot(second, hid[...], preferred_element_type=F32)
    for q in range(SPAN):
        wgt[r, n0 + q, 0] = w[:, 128 * q : 128 * q + 128]
        wgt[r, n0 + q, 1] = w[:, 128 * (SPAN + q) : 128 * (SPAN + q) + 128]


STAGES = ((0, 2), (2, 6), (6, 9))


def gather(r, stage, step, place, fx, got):
    n0 = step * 2
    first, last = STAGES[stage]
    ids = lax.broadcasted_iota(jnp.int32, (128, 128), 0).astype(F32).astype(BF16)
    halves = []
    for q in range(2):
        at = place[r, pl.ds(n0 + q, 16, stride=0), :]
        j = (at & 127).astype(F32)
        kk = at >> 7
        pieces = []
        for b in range(first, last):
            val = jnp.where(kk == b, j, -1.0).astype(BF16)
            val = jnp.concatenate([val] * 8, axis=0)
            pieces.append(jnp.where(val == ids, jnp.ones((), BF16), jnp.zeros((), BF16)))
        halves.append(jnp.concatenate(pieces, axis=0))
    hot = jnp.concatenate(halves, axis=1)
    rows = [fx[block_at(r, b)] for b in range(first, last)]
    out = jnp.dot(jnp.concatenate(rows, axis=1), hot, preferred_element_type=F32)
    for q in range(2):
        part = out[:, 128 * q : 128 * q + 128]
        got[r, n0 + q] = part if stage == 0 else got[r, n0 + q] + part


def hot_rows(r, place, hot_t):
    j = (place[r] & 127).astype(F32)
    cols = jnp.concatenate([j, jnp.zeros((104, 128), F32)], axis=0).T
    ids = lax.broadcasted_iota(jnp.int32, (128, 128), 1).astype(F32)
    for n in range(24):
        same = jnp.broadcast_to(cols[:, n : n + 1], (128, 128)) == ids
        hot_t[r, 128 * n : 128 * n + 128, :] = jnp.where(same, 1.0, 0.0).astype(BF16)


def row8(ref, r, q, n, times=1):
    v = ref[r, q, pl.ds(n, 8, stride=0), :]
    return v if times == 1 else jnp.concatenate([v] * times, axis=0)


TILE = 16


def aggregate(step, geo, wgt, got, agg):
    per = 64 // TILE
    r = step // per
    c0 = pl.multiple_of((step % per) * TILE, TILE)

    def body(n, acc):
        acc = list(acc)
        y = [None] + [row8(geo, r, q, n, TILE // 8) for q in range(8)]
        x = [got[r, n, pl.ds(m * 64 + c0, TILE), :] for m in range(9)]
        w = [wgt[r, n, 0, pl.ds(p * 64 + c0, TILE), :] for p in range(3)]
        p0 = w[0] * x[0]
        v = x[1] * y[1] + x[2] * y[2] + x[3] * y[3]
        acc[0] += p0 + w[1] * x[0] + w[2] * v
        for m in range(1, 9):
            acc[m] += p0 * y[m] + w[1] * x[m]
        return tuple(acc)

    acc = lax.fori_loop(0, 24, body, (jnp.zeros((TILE, 128), F32),) * 9, unroll=8)
    for m in range(9):
        agg[r, m, pl.ds(c0, TILE), :] = acc[m]


def readout(agg, read3, read_t3, w_out, energies):
    inv = []
    for r in range(2):
        a = [agg[r, m] for m in range(9)]
        sq = [v * v for v in a]
        inv.append(
            jnp.concatenate(
                [sq[0], sq[1] + sq[2] + sq[3], sq[4] + sq[5] + sq[6] + sq[7] + sq[8]], axis=0
            )
        )
    s = jnp.concatenate(inv, axis=1)
    hi, lo = split(s)
    z = jnp.dot(read3, jnp.concatenate([hi, lo, hi], axis=0), preferred_element_type=F32)
    sig = sigmoid(z)
    act = z * sig
    energy = jnp.sum(w_out * act, axis=0, keepdims=True)
    energies[0] = energy[:, :128]
    energies[1] = energy[:, 128:]
    gz = w_out * (sig + act * (1.0 - sig))
    hi, lo = split(gz)
    gs = jnp.dot(read_t3, jnp.concatenate([hi, lo, hi], axis=0), preferred_element_type=F32)
    gs = gs + gs
    for r in range(2):
        g = gs[:, 128 * r : 128 * r + 128]
        for m in range(9):
            part = 0 if m == 0 else 1 if m < 4 else 2
            agg[r, m] = agg[r, m] * g[64 * part : 64 * part + 64]


def backward(step, geo, wgt, got, agg, slopes):
    r = step // 24
    n = step % 24
    y = [None] + [row8(geo, r, q, n) for q in range(8)]
    acc = [jnp.zeros((8, 128), F32)] * 9
    for c in range(8):
        x = [got[r, n, m * 64 + 8 * c : m * 64 + 8 * c + 8, :] for m in range(9)]
        g = [agg[r, m, 8 * c : 8 * c + 8, :] for m in range(9)]
        w0, _, w2 = [wgt[r, n, 0, p * 64 + 8 * c : p * 64 + 8 * c + 8, :] for p in range(3)]
        d0, d1, d2 = [wgt[r, n, 1, p * 64 + 8 * c : p * 64 + 8 * c + 8, :] for p in range(3)]
        gx = g[0] * x[0]
        gy = g[0]
        for m in range(1, 9):
            gx += g[m] * x[m]
            gy += g[m] * y[m]
        v = x[1] * y[1] + x[2] * y[2] + x[3] * y[3]
        acc[0] += d1 * gx + d0 * (gy * x[0]) + d2 * (g[0] * v)
        p0 = w0 * x[0]
        p2 = w2 * g[0]
        for m in range(1, 9):
            acc[m] += p0 * g[m] + p2 * x[m] if m < 4 else p0 * g[m]
    for q in range(9):
        slopes[r, q, pl.ds(n, 1), :] = jnp.sum(acc[q], axis=0, keepdims=True)


def edge_forces(r, geo, unit, slopes, edge):
    r3, r5, r15 = math.sqrt(3.0), math.sqrt(5.0), math.sqrt(15.0)
    ux, uy, uz = (unit[r, q] for q in range(3))
    rinv = geo[r, 9]
    gd, g1, g2, g3, g4, g5, g6, g7, g8 = (slopes[r, q] for q in range(9))
    gx = r3 * g1 + r15 * (uy * g4 + uz * g7 + ux * g8)
    gy = r3 * g2 + r15 * (ux * g4 + uz * g5 - uy * g8)
    gz = r3 * g3 + r15 * (uy * g5 + ux * g7) + (3.0 * r5) * uz * g6
    along = gd - (gx * ux + gy * uy + gz * uz) * rinv
    out = []
    for q, (g, u) in enumerate(((gx, ux), (gy, uy), (gz, uz))):
        f = g * rinv + along * u
        edge[q] = f
        out.append(jnp.sum(f, axis=0, keepdims=True))
    return out


def scatter(r, place, edge, lhs, hot_t, centre, forces):
    pick = lax.broadcasted_iota(jnp.int32, (8, 128), 0)

    def body(n, carry):
        kk = place[r, pl.ds(n, 8, stride=0), :] >> 7
        value = jnp.zeros((8, 128), F32)
        for q in range(3):
            f = edge[q, pl.ds(n, 8, stride=0), :]
            hi = f.astype(BF16).astype(F32)
            value = jnp.where(pick == q, hi, jnp.where(pick == q + 3, f - hi, value))
        rows = [jnp.where(kk == b, value, 0.0) for b in range(9)] + [jnp.zeros((8, 128), F32)]
        lanes = pl.ds(pl.multiple_of(n * 128, 128), 128)
        lhs[:, lanes] = jnp.concatenate(rows, axis=0).astype(BF16)
        return carry

    lax.fori_loop(0, 24, body, 0, unroll=4)
    out = jnp.dot(lhs[...], hot_t[r], preferred_element_type=F32)
    for b in range(9):
        row, role = block_at(r, b)
        for q in range(3):
            v = -(out[8 * b + q : 8 * b + q + 1] + out[8 * b + q + 3 : 8 * b + q + 4])
            if row == r + 1 and role == 0:
                v += centre[q]
            forces[role, row, q] += v


def stack(w, axis):
    hi, lo = split(w)
    return jnp.concatenate([hi, hi, lo], axis=axis)


POS = 0
VEL = 8
OWN = 9
CHIP = 13
OFF = 14
CORNER = 15
FAR = 17
NEAR_CHIP = 21
FAR_CHIP = 22
FAR_CORNER = 23
TAIL = 25
COPIES = 30
AROUND = ((-1, -1), (-1, 0), (-1, 1), (0, -1), (0, 1), (1, -1), (1, 0), (1, 1))
BACK = ((0, 1), (0, -1), (-1, 1), (-1, 0), (-1, -1))


def step_kernel(
    positions_in, velocities_in, features, codes_in, counts_in, w_first_in, w_second_in, w_read_in,
    w_out_in, fresh_pos_in, fresh_vel_in, energies, new_pos, new_vel,
    positions, velocities, codes, counts, w_first, w_second, w_read, w_out, fresh_pos, fresh_vel,
    pos, vel_in, fx, place, geo, unit, basis, hid, wgt, got, agg, slopes, edge, lhs, hot_t,
    forces, tail, first, second, read3, read_t3, out_col, own_sem, load_sem, send_sem, recv_sem,
):
    s = lax.axis_index("shock")
    t = lax.axis_index("trans")
    ns = lax.axis_size("shock")
    nt = lax.axis_size("trans")
    core = lax.rem(s, 2)
    way = 1 - 2 * lax.rem(t, 2)
    out_way = 2 * core - 1

    def at(ds, dt):
        return (lax.rem(s + ds + ns, ns), lax.rem(t + dt + nt, nt))

    def copy(k, src, dst, to):
        return pltpu.make_async_remote_copy(
            src_ref=src,
            dst_ref=dst,
            send_sem=send_sem.at[k],
            recv_sem=recv_sem.at[k],
            device_id=to,
            device_id_type=pl.DeviceIdType.MESH,
        )

    barrier = pltpu.get_barrier_semaphore()
    for ds, dt in AROUND + ((0, 2), (0, -2)):
        pl.semaphore_signal(
            barrier, inc=1, device_id=at(ds, dt), device_id_type=pl.DeviceIdType.MESH
        )
    own = pltpu.make_async_copy(features.at[:, 0], fx.at[pl.ds(1, 2), 0], own_sem)
    loads = [
        pltpu.make_async_copy(src, dst, load_sem.at[i])
        for i, (src, dst) in enumerate(
            (
                (codes_in, codes),
                (positions_in, positions),
                (counts_in, counts),
                (w_first_in, w_first),
                (w_second_in, w_second),
                (w_read_in, w_read),
                (w_out_in, w_out),
                (velocities_in, velocities),
                (fresh_pos_in, fresh_pos),
                (fresh_vel_in, fresh_vel),
                (positions_in, pos.at[pl.ds(1, 2), 0]),
            )
        )
    ]
    own.start()
    for load in loads:
        load.start()
    pl.semaphore_wait(barrier, 10)

    flights = {}

    def role(dt):
        return 0 if dt == 0 else (3 - dt * way) // 2

    for i, (ds, dt) in enumerate(AROUND):
        if ds == 0:
            src, dst = positions_in, pos.at[pl.ds(1, 2), role(dt)]
        elif ds == 1:
            src, dst = positions_in.at[1], pos.at[0, role(dt)]
        else:
            src, dst = positions_in.at[0], pos.at[3, role(dt)]
        flights[POS + i] = copy(POS + i, src, dst, at(ds, dt))
    flights[VEL] = copy(VEL, velocities_in.at[0], vel_in, at(-1, 0))
    chip_row, chip_ghost = 1 - core, 3 * core
    off_row, off_ghost = core, 3 * (1 - core)
    order = (chip_row, off_row)
    my_off_ghost = 3 * core
    for i in range(4):
        row, half = 1 + order[i // 2], pl.ds(288 * (i % 2), 288)
        flights[OWN + i] = copy(
            OWN + i, features.at[row - 1, 0, half], fx.at[row, 1, half], at(0, way)
        )
        flights[FAR + i] = copy(
            FAR + i, fx.at[row, 1, half], fx.at[row, 2, half], at(0, 2 * way)
        )
    flights[CHIP] = copy(CHIP, features.at[chip_row, 0], fx.at[chip_ghost, 0], at(-out_way, 0))
    flights[OFF] = copy(OFF, features.at[off_row, 0], fx.at[off_ghost, 0], at(out_way, 0))
    for i in range(2):
        half = pl.ds(288 * i, 288)
        flights[CORNER + i] = copy(
            CORNER + i, features.at[off_row, 0, half], fx.at[off_ghost, 1, half], at(out_way, way)
        )
        flights[FAR_CORNER + i] = copy(
            FAR_CORNER + i, fx.at[my_off_ghost, 1, half], fx.at[my_off_ghost, 2, half], at(0, 2 * way)
        )
    for k in [OWN, *range(POS, POS + 8), *range(OWN + 1, OWN + 4), CHIP, CORNER, CORNER + 1, OFF, VEL]:
        flights[k].start()
    flights[NEAR_CHIP] = copy(
        NEAR_CHIP, fx.at[1 + chip_row, 1], fx.at[chip_ghost, 1], at(-out_way, 0)
    )
    flights[FAR_CHIP] = copy(
        FAR_CHIP, fx.at[1 + chip_row, 2], fx.at[chip_ghost, 2], at(-out_way, 0)
    )

    def gather_stage(r, stage):
        def gather_step(step, carry):
            gather(r, stage, step, place, fx, got)
            return carry

        lax.fori_loop(0, 12, gather_step, 0, unroll=6)

    def pass_on(k, to):
        flights[k].wait_recv()
        flights[to].start()

    loads[0].wait()
    for r in range(2):
        places(r, way, codes, place)
    own.wait()
    gather_stage(0, 0)
    gather_stage(1, 0)
    pass_on(OWN, FAR)

    for load in loads[1:]:
        load.wait()
    first[...] = jnp.concatenate([stack(w_first[...].T, 1), jnp.zeros((64, 8), BF16)], axis=1)
    second[...] = stack(w_second[...].T, 1)
    read3[...] = stack(w_read[...].T, 1)
    read_t3[...] = stack(w_read[...], 1)
    col = jnp.broadcast_to(w_out[...], (128, 128)).T
    out_col[...] = jnp.concatenate([col, col], axis=1)
    hot_rows(0, place, hot_t)
    pass_on(OWN + 1, FAR + 1)
    flights[NEAR_CHIP].start()
    hot_rows(1, place, hot_t)

    for k in range(POS, POS + 8):
        flights[k].wait_recv()

    @pl.when(s == 0)
    def _():
        pos[0] = jnp.zeros((3, 3, 1, 128), F32)

    @pl.when(s == ns - 1)
    def _():
        pos[3] = jnp.zeros((3, 3, 1, 128), F32)

    for r in range(2):
        geometry(r, pos, codes, place, counts, geo, unit)

    def radial_step(step, carry):
        radial(step, geo, first[...], second[...], basis, hid, wgt)
        return carry

    pass_on(OWN + 2, FAR + 2)
    lax.fori_loop(0, 24 // SPAN, radial_step, 0)
    pass_on(OWN + 3, FAR + 3)
    lax.fori_loop(24 // SPAN, 48 // SPAN, radial_step, 0)
    flights[FAR].wait_recv()
    flights[FAR + 1].wait_recv()
    flights[FAR_CHIP].start()
    pass_on(CORNER, FAR_CORNER)
    flights[CHIP].wait_recv()
    flights[NEAR_CHIP].wait_recv()
    gather_stage(1 - core, 1)
    pass_on(CORNER + 1, FAR_CORNER + 1)
    flights[OFF].wait_recv()
    for i in range(2):
        flights[FAR_CORNER + i].wait_send()
    blank = jnp.zeros((576, 128), BF16)

    def close(role):
        @pl.when(s == 0)
        def _():
            fx[0, role] = blank

        @pl.when(s == ns - 1)
        def _():
            fx[3, role] = blank

    close(0)
    close(1)
    gather_stage(core, 1)
    for k in (FAR + 2, FAR + 3, FAR_CHIP):
        flights[k].wait_recv()
    gather_stage(1 - core, 2)
    for i in range(2):
        flights[FAR_CORNER + i].wait_recv()
    close(2)
    gather_stage(core, 2)

    def aggregate_step(step, carry):
        aggregate(step, geo, wgt, got, agg)
        return carry

    lax.fori_loop(0, 2 * (64 // TILE), aggregate_step, 0)
    readout(agg, read3[...], read_t3[...], out_col[...], energies)

    def backward_step(step, carry):
        backward(step, geo, wgt, got, agg, slopes)
        return carry

    lax.fori_loop(0, 48, backward_step, 0, unroll=4)
    forces[...] = jnp.zeros_like(forces)
    for r in range(2):
        centre = edge_forces(r, geo, unit, slopes, edge)
        scatter(r, place, edge, lhs, hot_t, centre, forces)

    for i, (ds, dt) in enumerate(BACK):
        src = forces.at[role(dt), pl.ds(2 if ds == 0 else 0, 2)]
        flights[TAIL + i] = copy(TAIL + i, src, tail.at[i], at(ds, dt))
        flights[TAIL + i].start()
    for k in list(range(FAR_CORNER)):
        flights[k].wait_send()
    flights[VEL].wait_recv()
    for i in range(5):
        flights[TAIL + i].wait_recv()
    front = s == ns - 1
    above = tail[2] + tail[3] + tail[4]
    force = forces[0, 2:4] + tail[0] + tail[1] + jnp.where(front, 0.0, above)
    vel = velocities[1] + KICK_FACTOR * force[0]
    new_vel[0] = vel
    new_pos[0] = positions[1] + MOVE_FACTOR * vel
    vel = vel_in[...] + KICK_FACTOR * force[1]
    new_vel[1] = jnp.where(front, fresh_vel[...], vel)
    new_pos[1] = jnp.where(front, fresh_pos[...], pos[3, 0] + MOVE_FACTOR * vel)
    for i in range(5):
        flights[TAIL + i].wait_send()


def local(
    positions, velocities, features, neighbours, counts, w_first, w_second, w_read, w_out,
    fresh_positions, fresh_velocities,
):
    vmem = pl.BlockSpec(memory_space=pltpu.VMEM)
    whole = pl.BlockSpec(memory_space=pl.ANY)
    energies, new_pos, new_vel = pl.pallas_call(
        step_kernel,
        out_shape=(
            jax.ShapeDtypeStruct((2, 1, 128), F32),
            jax.ShapeDtypeStruct((2, 3, 1, 128), F32),
            jax.ShapeDtypeStruct((2, 3, 1, 128), F32),
        ),
        in_specs=[whole] * 11,
        out_specs=(vmem, vmem, vmem),
        scratch_shapes=[
            pltpu.VMEM((2, 3, 1, 128), F32),
            pltpu.VMEM((2, 3, 1, 128), F32),
            pltpu.VMEM((2, 1, 24, 128), jnp.int32),
            pltpu.VMEM((2, 1, 128), jnp.int32),
            pltpu.VMEM((8, 64), F32),
            pltpu.VMEM((64, 192), F32),
            pltpu.VMEM((192, 128), F32),
            pltpu.VMEM((1, 128), F32),
            pltpu.VMEM((3, 1, 128), F32),
            pltpu.VMEM((3, 1, 128), F32),
            pltpu.VMEM((4, 3, 3, 1, 128), F32),
            pltpu.VMEM((3, 1, 128), F32),
            pltpu.VMEM((4, 3, 576, 128), BF16),
            pltpu.VMEM((2, 24, 128), jnp.int32),
            pltpu.VMEM((2, GEO, 24, 128), F32),
            pltpu.VMEM((2, 3, 24, 128), F32),
            pltpu.VMEM((32, 256 * SPAN), BF16),
            pltpu.VMEM((192, 256 * SPAN), BF16),
            pltpu.VMEM((2, 24, 2, 192, 128), F32),
            pltpu.VMEM((2, 24, 576, 128), F32),
            pltpu.VMEM((2, 9, 64, 128), F32),
            pltpu.VMEM((2, 9, 24, 128), F32),
            pltpu.VMEM((3, 24, 128), F32),
            pltpu.VMEM((80, 3072), BF16),
            pltpu.VMEM((2, 3072, 128), BF16),
            pltpu.VMEM((3, 4, 3, 1, 128), F32),
            pltpu.VMEM((5, 2, 3, 1, 128), F32),
            pltpu.VMEM((64, 32), BF16),
            pltpu.VMEM((192, 192), BF16),
            pltpu.VMEM((128, 576), BF16),
            pltpu.VMEM((192, 384), BF16),
            pltpu.VMEM((128, 256), F32),
            pltpu.SemaphoreType.DMA,
            pltpu.SemaphoreType.DMA((11,)),
            pltpu.SemaphoreType.DMA((COPIES,)),
            pltpu.SemaphoreType.DMA((COPIES,)),
        ],
        compiler_params=pltpu.CompilerParams(
            vmem_limit_bytes=56 << 20, collective_id=0, has_side_effects=True
        ),
        name="step",
    )(
        positions.transpose(0, 2, 1, 3), velocities.transpose(0, 2, 1, 3), features, neighbours,
        counts, w_first.T, w_second.T, w_read.T, w_out[None],
        fresh_positions.transpose(1, 0, 2), fresh_velocities.transpose(1, 0, 2),
    )
    return energies, new_pos.transpose(0, 2, 1, 3), new_vel.transpose(0, 2, 1, 3)


def solution(mesh):
    spec = P("shock", "trans", None, None)
    return jax.shard_map(
        local,
        mesh=mesh,
        in_specs=(
            spec, spec, spec, spec, P("shock", "trans", None), P(), P(), P(), P(),
            P("trans", None, None), P("trans", None, None),
        ),
        out_specs=(P("shock", "trans", None), spec, spec),
        check_vma=False,
    )
```

```python
import math

import jax
import jax.numpy as jnp
from jax import lax
from jax.experimental import pallas as pl
from jax.experimental.pallas import tpu as pltpu
from jax.sharding import PartitionSpec as P

CUTOFF_RADIUS = 9.5
BLOCK_LENGTH = 13.2
KICK_FACTOR = 4.0
MOVE_FACTOR = 0.5
F32 = jnp.float32
BF16 = jnp.bfloat16
GEO = 12
SPAN = 24


def split(x):
    hi = x.astype(BF16)
    return hi, (x - hi.astype(F32)).astype(BF16)


def sigmoid(z):
    return 0.5 * jnp.tanh(0.5 * z) + 0.5


def sin_cos_pi(t):
    whole = jnp.floor(t + 0.5)
    half = whole * 0.5
    sign = 1.0 - 4.0 * (half - jnp.floor(half))
    r = (t - whole) * math.pi
    r2 = r * r
    s = r * (1.0 + r2 * (-1 / 6 + r2 * (1 / 120 + r2 * (-1 / 5040 + r2 * (1 / 362880 - r2 / 39916800)))))
    c = 1.0 + r2 * (
        -1 / 2 + r2 * (1 / 24 + r2 * (-1 / 720 + r2 * (1 / 40320 + r2 * (-1 / 3628800 + r2 / 479001600))))
    )
    return s * sign, c * sign


def block_at(r, kk):
    if kk < 2:
        return 1 + kk, 0
    if kk == 2:
        return 3 * r, 0
    return r + (kk - 3) % 3, (kk - 3) // 3 + 1


def places(r, way, codes, place):
    code = codes[r, 0]
    cell = code >> 7
    iz = (cell >= 9).astype(jnp.int32) + (cell >= 18).astype(jnp.int32)
    k = cell - 9 * iz
    is_ = (k >= 3).astype(jnp.int32) + (k >= 6).astype(jnp.int32)
    it = k - 3 * is_ - 1
    centre = jnp.where(is_ == 0, 2, is_ - 1) if r == 0 else is_
    kk = jnp.where(it == 0, centre, jnp.where(it == way, 3, 6) + is_)
    place[r] = kk * 128 + (code & 127)


def geometry(r, pos, codes, place, counts, geo, unit):
    for part in range(3):
        rows = slice(8 * part, 8 * part + 8)
        code = codes[r, 0, rows, :]
        j = code & 127
        cell = code >> 7
        iz = (cell >= 9).astype(jnp.int32) + (cell >= 18).astype(jnp.int32)
        k = cell - 9 * iz
        is_ = (k >= 3).astype(jnp.int32) + (k >= 6).astype(jnp.int32)
        it = k - 3 * is_
        kk = place[r, rows, :] >> 7
        shifts = [(v - 1).astype(F32) * BLOCK_LENGTH for v in (is_, it, iz)]
        delta = []
        for comp in range(3):
            other = jnp.zeros((8, 128), F32)
            for b in range(9):
                row, role = block_at(r, b)
                row = pos[row, role, comp, pl.ds(0, 8, stride=0), :]
                got = jnp.take_along_axis(row, j, axis=1, mode="promise_in_bounds")
                other = jnp.where(kk == b, got, other)
            centre = pos[r + 1, 0, comp, pl.ds(0, 8, stride=0), :]
            delta.append(other + shifts[comp] - centre)
        dx, dy, dz = delta
        d = jnp.sqrt(dx * dx + dy * dy + dz * dz)
        rinv = 1.0 / d
        ux, uy, uz = dx * rinv, dy * rinv, dz * rinv
        x = d * (1.0 / CUTOFF_RADIUS)
        x2 = x * x
        x4 = x2 * x2
        slot = lax.broadcasted_iota(jnp.int32, (8, 128), 0) + 8 * part
        live = jnp.where(slot < counts[r, pl.ds(0, 8, stride=0), :], 1.0 / 24.0, 0.0)
        env = (1.0 + x4 * x2 * (-28.0 + x * (48.0 - 21.0 * x))) * live
        slope = (-168.0 / CUTOFF_RADIUS) * x4 * x * ((1.0 - x) * (1.0 - x)) * live
        r3, r5, r15 = math.sqrt(3.0), math.sqrt(5.0), math.sqrt(15.0)
        values = [
            r3 * ux,
            r3 * uy,
            r3 * uz,
            r15 * ux * uy,
            r15 * uy * uz,
            0.5 * r5 * (3.0 * uz * uz - 1.0),
            r15 * ux * uz,
            0.5 * r15 * (ux * ux - uy * uy),
            x,
            rinv,
            env,
            slope,
        ]
        for q, v in enumerate(values):
            geo[r, q, rows, :] = v
        for q, v in enumerate((ux, uy, uz)):
            unit[r, q, rows, :] = v


def radial(step, geo, first, second, basis, hid, wgt):
    per = 24 // SPAN
    r = step // per
    n0 = (step % per) * SPAN
    order = (lax.broadcasted_iota(jnp.int32, (8, 128), 0) + 1).astype(F32)
    scale = math.sqrt(2.0 / CUTOFF_RADIUS)
    zero8 = jnp.zeros((8, 128), F32)
    for q in range(SPAN):
        x = geo[r, 8, pl.ds(n0 + q, 8, stride=0), :]
        rinv = geo[r, 9, pl.ds(n0 + q, 8, stride=0), :]
        s, c = sin_cos_pi(x * order)
        b = (scale * rinv) * s
        bd = rinv * ((scale * math.pi / CUTOFF_RADIUS) * order * c - b)
        for v, at in ((b, q), (bd, SPAN + q)):
            hi = v.astype(BF16).astype(F32)
            lanes = slice(128 * at, 128 * at + 128)
            basis[0:16, lanes] = jnp.concatenate([hi, v - hi], axis=0).astype(BF16)
            basis[16:32, lanes] = jnp.concatenate([hi, zero8], axis=0).astype(BF16)
    z = jnp.dot(first, basis[...], preferred_element_type=F32)
    for q in range(SPAN):
        env = geo[r, 10, pl.ds(n0 + q, 8, stride=0), :]
        slope = geo[r, 11, pl.ds(n0 + q, 8, stride=0), :]
        env, slope = (jnp.concatenate([v] * 8, axis=0) for v in (env, slope))
        zq = z[:, 128 * q : 128 * q + 128]
        zd = z[:, 128 * (SPAN + q) : 128 * (SPAN + q) + 128]
        sig = sigmoid(zq)
        act = zq * sig
        h = act * env
        hd = (sig + act * (1.0 - sig)) * zd * env + act * slope
        for v, at in ((h, q), (hd, SPAN + q)):
            hi, lo = split(v)
            lanes = slice(128 * at, 128 * at + 128)
            hid[0:64, lanes] = hi
            hid[64:128, lanes] = lo
            hid[128:192, lanes] = hi
    w = jnp.dot(second, hid[...], preferred_element_type=F32)
    for q in range(SPAN):
        wgt[r, n0 + q, 0] = w[:, 128 * q : 128 * q + 128]
        wgt[r, n0 + q, 1] = w[:, 128 * (SPAN + q) : 128 * (SPAN + q) + 128]


STAGES = ((0, 2), (2, 6), (6, 9))


def gather(r, stage, step, place, fx, got):
    n0 = step * 2
    first, last = STAGES[stage]
    ids = lax.broadcasted_iota(jnp.int32, (128, 128), 0).astype(F32).astype(BF16)
    halves = []
    for q in range(2):
        at = place[r, pl.ds(n0 + q, 16, stride=0), :]
        j = (at & 127).astype(F32)
        kk = at >> 7
        pieces = []
        for b in range(first, last):
            val = jnp.where(kk == b, j, -1.0).astype(BF16)
            val = jnp.concatenate([val] * 8, axis=0)
            pieces.append(jnp.where(val == ids, jnp.ones((), BF16), jnp.zeros((), BF16)))
        halves.append(jnp.concatenate(pieces, axis=0))
    hot = jnp.concatenate(halves, axis=1)
    rows = [fx[block_at(r, b)] for b in range(first, last)]
    out = jnp.dot(jnp.concatenate(rows, axis=1), hot, preferred_element_type=F32)
    for q in range(2):
        part = out[:, 128 * q : 128 * q + 128]
        got[r, n0 + q] = part if stage == 0 else got[r, n0 + q] + part


def hot_rows(r, place, hot_t):
    j = (place[r] & 127).astype(F32)
    cols = jnp.concatenate([j, jnp.zeros((104, 128), F32)], axis=0).T
    ids = lax.broadcasted_iota(jnp.int32, (128, 128), 1).astype(F32)
    for n in range(24):
        same = jnp.broadcast_to(cols[:, n : n + 1], (128, 128)) == ids
        hot_t[r, 128 * n : 128 * n + 128, :] = jnp.where(same, 1.0, 0.0).astype(BF16)


def row8(ref, r, q, n, times=1):
    v = ref[r, q, pl.ds(n, 8, stride=0), :]
    return v if times == 1 else jnp.concatenate([v] * times, axis=0)


TILE = 16


def aggregate(step, geo, wgt, got, agg):
    per = 64 // TILE
    r = step // per
    c0 = pl.multiple_of((step % per) * TILE, TILE)

    def body(n, acc):
        acc = list(acc)
        y = [None] + [row8(geo, r, q, n, TILE // 8) for q in range(8)]
        x = [got[r, n, pl.ds(m * 64 + c0, TILE), :] for m in range(9)]
        w = [wgt[r, n, 0, pl.ds(p * 64 + c0, TILE), :] for p in range(3)]
        p0 = w[0] * x[0]
        v = x[1] * y[1] + x[2] * y[2] + x[3] * y[3]
        acc[0] += p0 + w[1] * x[0] + w[2] * v
        for m in range(1, 9):
            acc[m] += p0 * y[m] + w[1] * x[m]
        return tuple(acc)

    acc = lax.fori_loop(0, 24, body, (jnp.zeros((TILE, 128), F32),) * 9, unroll=8)
    for m in range(9):
        agg[r, m, pl.ds(c0, TILE), :] = acc[m]


def readout(agg, read3, read_t3, w_out, energies):
    inv = []
    for r in range(2):
        a = [agg[r, m] for m in range(9)]
        sq = [v * v for v in a]
        inv.append(
            jnp.concatenate(
                [sq[0], sq[1] + sq[2] + sq[3], sq[4] + sq[5] + sq[6] + sq[7] + sq[8]], axis=0
            )
        )
    s = jnp.concatenate(inv, axis=1)
    hi, lo = split(s)
    z = jnp.dot(read3, jnp.concatenate([hi, lo, hi], axis=0), preferred_element_type=F32)
    sig = sigmoid(z)
    act = z * sig
    energy = jnp.sum(w_out * act, axis=0, keepdims=True)
    energies[0] = energy[:, :128]
    energies[1] = energy[:, 128:]
    gz = w_out * (sig + act * (1.0 - sig))
    hi, lo = split(gz)
    gs = jnp.dot(read_t3, jnp.concatenate([hi, lo, hi], axis=0), preferred_element_type=F32)
    gs = gs + gs
    for r in range(2):
        g = gs[:, 128 * r : 128 * r + 128]
        for m in range(9):
            part = 0 if m == 0 else 1 if m < 4 else 2
            agg[r, m] = agg[r, m] * g[64 * part : 64 * part + 64]


def backward(step, geo, wgt, got, agg, slopes):
    r = step // 24
    n = step % 24
    y = [None] + [row8(geo, r, q, n) for q in range(8)]
    acc = [jnp.zeros((8, 128), F32)] * 9
    for c in range(8):
        x = [got[r, n, m * 64 + 8 * c : m * 64 + 8 * c + 8, :] for m in range(9)]
        g = [agg[r, m, 8 * c : 8 * c + 8, :] for m in range(9)]
        w0, _, w2 = [wgt[r, n, 0, p * 64 + 8 * c : p * 64 + 8 * c + 8, :] for p in range(3)]
        d0, d1, d2 = [wgt[r, n, 1, p * 64 + 8 * c : p * 64 + 8 * c + 8, :] for p in range(3)]
        gx = g[0] * x[0]
        gy = g[0]
        for m in range(1, 9):
            gx += g[m] * x[m]
            gy += g[m] * y[m]
        v = x[1] * y[1] + x[2] * y[2] + x[3] * y[3]
        acc[0] += d1 * gx + d0 * (gy * x[0]) + d2 * (g[0] * v)
        p0 = w0 * x[0]
        p2 = w2 * g[0]
        for m in range(1, 9):
            acc[m] += p0 * g[m] + p2 * x[m] if m < 4 else p0 * g[m]
    for q in range(9):
        slopes[r, q, pl.ds(n, 1), :] = jnp.sum(acc[q], axis=0, keepdims=True)


def edge_forces(r, geo, unit, slopes, edge):
    r3, r5, r15 = math.sqrt(3.0), math.sqrt(5.0), math.sqrt(15.0)
    ux, uy, uz = (unit[r, q] for q in range(3))
    rinv = geo[r, 9]
    gd, g1, g2, g3, g4, g5, g6, g7, g8 = (slopes[r, q] for q in range(9))
    gx = r3 * g1 + r15 * (uy * g4 + uz * g7 + ux * g8)
    gy = r3 * g2 + r15 * (ux * g4 + uz * g5 - uy * g8)
    gz = r3 * g3 + r15 * (uy * g5 + ux * g7) + (3.0 * r5) * uz * g6
    along = gd - (gx * ux + gy * uy + gz * uz) * rinv
    out = []
    for q, (g, u) in enumerate(((gx, ux), (gy, uy), (gz, uz))):
        f = g * rinv + along * u
        edge[q] = f
        out.append(jnp.sum(f, axis=0, keepdims=True))
    return out


def scatter(r, place, edge, lhs, hot_t, centre, forces):
    pick = lax.broadcasted_iota(jnp.int32, (8, 128), 0)

    def body(n, carry):
        kk = place[r, pl.ds(n, 8, stride=0), :] >> 7
        value = jnp.zeros((8, 128), F32)
        for q in range(3):
            f = edge[q, pl.ds(n, 8, stride=0), :]
            hi = f.astype(BF16).astype(F32)
            value = jnp.where(pick == q, hi, jnp.where(pick == q + 3, f - hi, value))
        rows = [jnp.where(kk == b, value, 0.0) for b in range(9)] + [jnp.zeros((8, 128), F32)]
        lanes = pl.ds(pl.multiple_of(n * 128, 128), 128)
        lhs[:, lanes] = jnp.concatenate(rows, axis=0).astype(BF16)
        return carry

    lax.fori_loop(0, 24, body, 0, unroll=4)
    out = jnp.dot(lhs[...], hot_t[r], preferred_element_type=F32)
    for b in range(9):
        row, role = block_at(r, b)
        for q in range(3):
            v = -(out[8 * b + q : 8 * b + q + 1] + out[8 * b + q + 3 : 8 * b + q + 4])
            if row == r + 1 and role == 0:
                v += centre[q]
            forces[role, row, q] += v


def stack(w, axis):
    hi, lo = split(w)
    return jnp.concatenate([hi, hi, lo], axis=axis)


POS = 0
VEL = 8
OWN = 9
CHIP = 13
OFF = 14
CORNER = 15
FAR = 17
NEAR_CHIP = 21
FAR_CHIP = 22
FAR_CORNER = 23
TAIL = 25
COPIES = 30
AROUND = ((-1, -1), (-1, 0), (-1, 1), (0, -1), (0, 1), (1, -1), (1, 0), (1, 1))
BACK = ((0, 1), (0, -1), (-1, 1), (-1, 0), (-1, -1))


def step_kernel(
    positions_in, velocities_in, features, codes_in, counts_in, w_first_in, w_second_in, w_read_in,
    w_out_in, fresh_pos_in, fresh_vel_in, energies, new_pos, new_vel,
    positions, velocities, codes, counts, w_first, w_second, w_read, w_out, fresh_pos, fresh_vel,
    pos, vel_in, fx, place, geo, unit, basis, hid, wgt, got, agg, slopes, edge, lhs, hot_t,
    forces, tail, first, second, read3, read_t3, out_col, own_sem, load_sem, send_sem, recv_sem,
):
    s = lax.axis_index("shock")
    t = lax.axis_index("trans")
    ns = lax.axis_size("shock")
    nt = lax.axis_size("trans")
    core = lax.rem(s, 2)
    way = 1 - 2 * lax.rem(t, 2)
    out_way = 2 * core - 1

    def at(ds, dt):
        return (lax.rem(s + ds + ns, ns), lax.rem(t + dt + nt, nt))

    def copy(k, src, dst, to):
        return pltpu.make_async_remote_copy(
            src_ref=src,
            dst_ref=dst,
            send_sem=send_sem.at[k],
            recv_sem=recv_sem.at[k],
            device_id=to,
            device_id_type=pl.DeviceIdType.MESH,
        )

    barrier = pltpu.get_barrier_semaphore()
    for ds, dt in AROUND + ((0, 2), (0, -2)):
        pl.semaphore_signal(
            barrier, inc=1, device_id=at(ds, dt), device_id_type=pl.DeviceIdType.MESH
        )
    own = pltpu.make_async_copy(features.at[:, 0], fx.at[pl.ds(1, 2), 0], own_sem)
    loads = [
        pltpu.make_async_copy(src, dst, load_sem.at[i])
        for i, (src, dst) in enumerate(
            (
                (codes_in, codes),
                (positions_in, positions),
                (counts_in, counts),
                (w_first_in, w_first),
                (w_second_in, w_second),
                (w_read_in, w_read),
                (w_out_in, w_out),
                (velocities_in, velocities),
                (fresh_pos_in, fresh_pos),
                (fresh_vel_in, fresh_vel),
                (positions_in, pos.at[pl.ds(1, 2), 0]),
            )
        )
    ]
    own.start()
    for load in loads:
        load.start()
    pl.semaphore_wait(barrier, 10)

    flights = {}

    def role(dt):
        return 0 if dt == 0 else (3 - dt * way) // 2

    for i, (ds, dt) in enumerate(AROUND):
        if ds == 0:
            src, dst = positions_in, pos.at[pl.ds(1, 2), role(dt)]
        elif ds == 1:
            src, dst = positions_in.at[1], pos.at[0, role(dt)]
        else:
            src, dst = positions_in.at[0], pos.at[3, role(dt)]
        flights[POS + i] = copy(POS + i, src, dst, at(ds, dt))
    flights[VEL] = copy(VEL, velocities_in.at[0], vel_in, at(-1, 0))
    chip_row, chip_ghost = 1 - core, 3 * core
    off_row, off_ghost = core, 3 * (1 - core)
    order = (chip_row, off_row)
    my_off_ghost = 3 * core
    for i in range(4):
        row, half = 1 + order[i // 2], pl.ds(288 * (i % 2), 288)
        flights[OWN + i] = copy(
            OWN + i, features.at[row - 1, 0, half], fx.at[row, 1, half], at(0, way)
        )
        flights[FAR + i] = copy(
            FAR + i, fx.at[row, 1, half], fx.at[row, 2, half], at(0, 2 * way)
        )
    flights[CHIP] = copy(CHIP, features.at[chip_row, 0], fx.at[chip_ghost, 0], at(-out_way, 0))
    flights[OFF] = copy(OFF, features.at[off_row, 0], fx.at[off_ghost, 0], at(out_way, 0))
    for i in range(2):
        half = pl.ds(288 * i, 288)
        flights[CORNER + i] = copy(
            CORNER + i, features.at[off_row, 0, half], fx.at[off_ghost, 1, half], at(out_way, way)
        )
        flights[FAR_CORNER + i] = copy(
            FAR_CORNER + i, fx.at[my_off_ghost, 1, half], fx.at[my_off_ghost, 2, half], at(0, 2 * way)
        )
    for k in [OWN, *range(POS, POS + 8), *range(OWN + 1, OWN + 4), CHIP, CORNER, CORNER + 1, OFF, VEL]:
        flights[k].start()
    flights[NEAR_CHIP] = copy(
        NEAR_CHIP, fx.at[1 + chip_row, 1], fx.at[chip_ghost, 1], at(-out_way, 0)
    )
    flights[FAR_CHIP] = copy(
        FAR_CHIP, fx.at[1 + chip_row, 2], fx.at[chip_ghost, 2], at(-out_way, 0)
    )

    def gather_stage(r, stage, first_step=0, last_step=12):
        def gather_step(step, carry):
            gather(r, stage, step, place, fx, got)
            return carry

        lax.fori_loop(first_step, last_step, gather_step, 0, unroll=6)

    def pass_on(k, to):
        flights[k].wait_recv()
        flights[to].start()

    loads[0].wait()
    for r in range(2):
        places(r, way, codes, place)
    own.wait()
    gather_stage(0, 0)
    gather_stage(1, 0)
    pass_on(OWN, FAR)

    for load in loads[1:]:
        load.wait()
    first[...] = jnp.concatenate([stack(w_first[...].T, 1), jnp.zeros((64, 8), BF16)], axis=1)
    second[...] = stack(w_second[...].T, 1)
    read3[...] = stack(w_read[...].T, 1)
    read_t3[...] = stack(w_read[...], 1)
    col = jnp.broadcast_to(w_out[...], (128, 128)).T
    out_col[...] = jnp.concatenate([col, col], axis=1)
    hot_rows(0, place, hot_t)
    pass_on(OWN + 1, FAR + 1)
    flights[NEAR_CHIP].start()
    hot_rows(1, place, hot_t)

    for k in range(POS, POS + 8):
        flights[k].wait_recv()

    @pl.when(s == 0)
    def _():
        pos[0] = jnp.zeros((3, 3, 1, 128), F32)

    @pl.when(s == ns - 1)
    def _():
        pos[3] = jnp.zeros((3, 3, 1, 128), F32)

    for r in range(2):
        geometry(r, pos, codes, place, counts, geo, unit)

    def radial_step(step, carry):
        radial(step, geo, first[...], second[...], basis, hid, wgt)
        return carry

    pass_on(OWN + 2, FAR + 2)
    lax.fori_loop(0, 24 // SPAN, radial_step, 0)
    pass_on(OWN + 3, FAR + 3)
    lax.fori_loop(24 // SPAN, 48 // SPAN, radial_step, 0)
    flights[FAR].wait_recv()
    flights[FAR + 1].wait_recv()
    flights[FAR_CHIP].start()
    pass_on(CORNER, FAR_CORNER)
    flights[CHIP].wait_recv()
    flights[NEAR_CHIP].wait_recv()
    gather_stage(1 - core, 1, 0, 6)
    pass_on(CORNER + 1, FAR_CORNER + 1)
    gather_stage(1 - core, 1, 6, 12)
    flights[OFF].wait_recv()
    for i in range(2):
        flights[FAR_CORNER + i].wait_send()
    blank = jnp.zeros((576, 128), BF16)

    def close(role):
        @pl.when(s == 0)
        def _():
            fx[0, role] = blank

        @pl.when(s == ns - 1)
        def _():
            fx[3, role] = blank

    close(0)
    close(1)
    gather_stage(core, 1)
    for k in (FAR + 2, FAR + 3, FAR_CHIP):
        flights[k].wait_recv()
    gather_stage(1 - core, 2)

    def aggregate_row(r):
        def aggregate_step(step, carry):
            aggregate(r * (64 // TILE) + step, geo, wgt, got, agg)
            return carry

        lax.fori_loop(0, 64 // TILE, aggregate_step, 0)

    aggregate_row(1 - core)
    for i in range(2):
        flights[FAR_CORNER + i].wait_recv()
    close(2)
    gather_stage(core, 2)
    aggregate_row(core)
    readout(agg, read3[...], read_t3[...], out_col[...], energies)

    def backward_step(step, carry):
        backward(step, geo, wgt, got, agg, slopes)
        return carry

    lax.fori_loop(0, 48, backward_step, 0, unroll=4)
    forces[...] = jnp.zeros_like(forces)
    for r in range(2):
        centre = edge_forces(r, geo, unit, slopes, edge)
        scatter(r, place, edge, lhs, hot_t, centre, forces)

    for i, (ds, dt) in enumerate(BACK):
        src = forces.at[role(dt), pl.ds(2 if ds == 0 else 0, 2)]
        flights[TAIL + i] = copy(TAIL + i, src, tail.at[i], at(ds, dt))
        flights[TAIL + i].start()
    for k in list(range(FAR_CORNER)):
        flights[k].wait_send()
    flights[VEL].wait_recv()
    for i in range(5):
        flights[TAIL + i].wait_recv()
    front = s == ns - 1
    above = tail[2] + tail[3] + tail[4]
    force = forces[0, 2:4] + tail[0] + tail[1] + jnp.where(front, 0.0, above)
    vel = velocities[1] + KICK_FACTOR * force[0]
    new_vel[0] = vel
    new_pos[0] = positions[1] + MOVE_FACTOR * vel
    vel = vel_in[...] + KICK_FACTOR * force[1]
    new_vel[1] = jnp.where(front, fresh_vel[...], vel)
    new_pos[1] = jnp.where(front, fresh_pos[...], pos[3, 0] + MOVE_FACTOR * vel)
    for i in range(5):
        flights[TAIL + i].wait_send()


def local(
    positions, velocities, features, neighbours, counts, w_first, w_second, w_read, w_out,
    fresh_positions, fresh_velocities,
):
    vmem = pl.BlockSpec(memory_space=pltpu.VMEM)
    whole = pl.BlockSpec(memory_space=pl.ANY)
    energies, new_pos, new_vel = pl.pallas_call(
        step_kernel,
        out_shape=(
            pltpu.VMEM((2, 1, 128), F32),
            pltpu.VMEM((2, 3, 1, 128), F32),
            pltpu.VMEM((2, 3, 1, 128), F32),
        ),
        in_specs=[whole] * 11,
        out_specs=(vmem, vmem, vmem),
        scratch_shapes=[
            pltpu.VMEM((2, 3, 1, 128), F32),
            pltpu.VMEM((2, 3, 1, 128), F32),
            pltpu.VMEM((2, 1, 24, 128), jnp.int32),
            pltpu.VMEM((2, 1, 128), jnp.int32),
            pltpu.VMEM((8, 64), F32),
            pltpu.VMEM((64, 192), F32),
            pltpu.VMEM((192, 128), F32),
            pltpu.VMEM((1, 128), F32),
            pltpu.VMEM((3, 1, 128), F32),
            pltpu.VMEM((3, 1, 128), F32),
            pltpu.VMEM((4, 3, 3, 1, 128), F32),
            pltpu.VMEM((3, 1, 128), F32),
            pltpu.VMEM((4, 3, 576, 128), BF16),
            pltpu.VMEM((2, 24, 128), jnp.int32),
            pltpu.VMEM((2, GEO, 24, 128), F32),
            pltpu.VMEM((2, 3, 24, 128), F32),
            pltpu.VMEM((32, 256 * SPAN), BF16),
            pltpu.VMEM((192, 256 * SPAN), BF16),
            pltpu.VMEM((2, 24, 2, 192, 128), F32),
            pltpu.VMEM((2, 24, 576, 128), F32),
            pltpu.VMEM((2, 9, 64, 128), F32),
            pltpu.VMEM((2, 9, 24, 128), F32),
            pltpu.VMEM((3, 24, 128), F32),
            pltpu.VMEM((80, 3072), BF16),
            pltpu.VMEM((2, 3072, 128), BF16),
            pltpu.VMEM((3, 4, 3, 1, 128), F32),
            pltpu.VMEM((5, 2, 3, 1, 128), F32),
            pltpu.VMEM((64, 32), BF16),
            pltpu.VMEM((192, 192), BF16),
            pltpu.VMEM((128, 576), BF16),
            pltpu.VMEM((192, 384), BF16),
            pltpu.VMEM((128, 256), F32),
            pltpu.SemaphoreType.DMA,
            pltpu.SemaphoreType.DMA((11,)),
            pltpu.SemaphoreType.DMA((COPIES,)),
            pltpu.SemaphoreType.DMA((COPIES,)),
        ],
        compiler_params=pltpu.CompilerParams(
            vmem_limit_bytes=56 << 20, collective_id=0, has_side_effects=True
        ),
        name="step",
    )(
        positions.transpose(0, 2, 1, 3), velocities.transpose(0, 2, 1, 3), features, neighbours,
        counts, w_first.T, w_second.T, w_read.T, w_out[None],
        fresh_positions.transpose(1, 0, 2), fresh_velocities.transpose(1, 0, 2),
    )
    return energies, new_pos.transpose(0, 2, 1, 3), new_vel.transpose(0, 2, 1, 3)


def solution(mesh):
    spec = P("shock", "trans", None, None)
    return jax.shard_map(
        local,
        mesh=mesh,
        in_specs=(
            spec, spec, spec, spec, P("shock", "trans", None), P(), P(), P(), P(),
            P("trans", None, None), P("trans", None, None),
        ),
        out_specs=(P("shock", "trans", None), spec, spec),
        check_vma=False,
    )
```

```python
import math

import jax
import jax.numpy as jnp
from jax import lax
from jax.experimental import pallas as pl
from jax.experimental.pallas import tpu as pltpu
from jax.sharding import PartitionSpec as P

CUTOFF_RADIUS = 9.5
BLOCK_LENGTH = 13.2
KICK_FACTOR = 4.0
MOVE_FACTOR = 0.5
F32 = jnp.float32
BF16 = jnp.bfloat16
GEO = 12
SPAN = 24


def split(x):
    hi = x.astype(BF16)
    return hi, (x - hi.astype(F32)).astype(BF16)


def sigmoid(z):
    return 0.5 * jnp.tanh(0.5 * z) + 0.5


def sin_cos_pi(t):
    whole = jnp.floor(t + 0.5)
    half = whole * 0.5
    sign = 1.0 - 4.0 * (half - jnp.floor(half))
    r = (t - whole) * math.pi
    r2 = r * r
    s = r * (1.0 + r2 * (-1 / 6 + r2 * (1 / 120 + r2 * (-1 / 5040 + r2 * (1 / 362880 - r2 / 39916800)))))
    c = 1.0 + r2 * (
        -1 / 2 + r2 * (1 / 24 + r2 * (-1 / 720 + r2 * (1 / 40320 + r2 * (-1 / 3628800 + r2 / 479001600))))
    )
    return s * sign, c * sign


def block_at(r, kk):
    if kk < 2:
        return 1 + kk, 0
    if kk == 2:
        return 3 * r, 0
    return r + (kk - 3) % 3, (kk - 3) // 3 + 1


def places(r, way, codes, place):
    code = codes[r, 0]
    cell = code >> 7
    iz = (cell >= 9).astype(jnp.int32) + (cell >= 18).astype(jnp.int32)
    k = cell - 9 * iz
    is_ = (k >= 3).astype(jnp.int32) + (k >= 6).astype(jnp.int32)
    it = k - 3 * is_ - 1
    centre = jnp.where(is_ == 0, 2, is_ - 1) if r == 0 else is_
    kk = jnp.where(it == 0, centre, jnp.where(it == way, 3, 6) + is_)
    place[r] = kk * 128 + (code & 127)


def geometry(r, pos, codes, place, counts, geo, unit):
    for part in range(3):
        rows = slice(8 * part, 8 * part + 8)
        code = codes[r, 0, rows, :]
        j = code & 127
        cell = code >> 7
        iz = (cell >= 9).astype(jnp.int32) + (cell >= 18).astype(jnp.int32)
        k = cell - 9 * iz
        is_ = (k >= 3).astype(jnp.int32) + (k >= 6).astype(jnp.int32)
        it = k - 3 * is_
        kk = place[r, rows, :] >> 7
        shifts = [(v - 1).astype(F32) * BLOCK_LENGTH for v in (is_, it, iz)]
        delta = []
        for comp in range(3):
            other = jnp.zeros((8, 128), F32)
            for b in range(9):
                row, role = block_at(r, b)
                row = pos[row, role, comp, pl.ds(0, 8, stride=0), :]
                got = jnp.take_along_axis(row, j, axis=1, mode="promise_in_bounds")
                other = jnp.where(kk == b, got, other)
            centre = pos[r + 1, 0, comp, pl.ds(0, 8, stride=0), :]
            delta.append(other + shifts[comp] - centre)
        dx, dy, dz = delta
        d = jnp.sqrt(dx * dx + dy * dy + dz * dz)
        rinv = 1.0 / d
        ux, uy, uz = dx * rinv, dy * rinv, dz * rinv
        x = d * (1.0 / CUTOFF_RADIUS)
        x2 = x * x
        x4 = x2 * x2
        slot = lax.broadcasted_iota(jnp.int32, (8, 128), 0) + 8 * part
        live = jnp.where(slot < counts[r, pl.ds(0, 8, stride=0), :], 1.0 / 24.0, 0.0)
        env = (1.0 + x4 * x2 * (-28.0 + x * (48.0 - 21.0 * x))) * live
        slope = (-168.0 / CUTOFF_RADIUS) * x4 * x * ((1.0 - x) * (1.0 - x)) * live
        r3, r5, r15 = math.sqrt(3.0), math.sqrt(5.0), math.sqrt(15.0)
        values = [
            r3 * ux,
            r3 * uy,
            r3 * uz,
            r15 * ux * uy,
            r15 * uy * uz,
            0.5 * r5 * (3.0 * uz * uz - 1.0),
            r15 * ux * uz,
            0.5 * r15 * (ux * ux - uy * uy),
            x,
            rinv,
            env,
            slope,
        ]
        for q, v in enumerate(values):
            geo[r, q, rows, :] = v
        for q, v in enumerate((ux, uy, uz)):
            unit[r, q, rows, :] = v


def radial(step, geo, first, second, basis, hid, wgt):
    per = 24 // SPAN
    r = step // per
    n0 = (step % per) * SPAN
    order = (lax.broadcasted_iota(jnp.int32, (8, 128), 0) + 1).astype(F32)
    scale = math.sqrt(2.0 / CUTOFF_RADIUS)
    zero8 = jnp.zeros((8, 128), F32)
    for q in range(SPAN):
        x = geo[r, 8, pl.ds(n0 + q, 8, stride=0), :]
        rinv = geo[r, 9, pl.ds(n0 + q, 8, stride=0), :]
        s, c = sin_cos_pi(x * order)
        b = (scale * rinv) * s
        bd = rinv * ((scale * math.pi / CUTOFF_RADIUS) * order * c - b)
        for v, at in ((b, q), (bd, SPAN + q)):
            hi = v.astype(BF16).astype(F32)
            lanes = slice(128 * at, 128 * at + 128)
            basis[0:16, lanes] = jnp.concatenate([hi, v - hi], axis=0).astype(BF16)
            basis[16:32, lanes] = jnp.concatenate([hi, zero8], axis=0).astype(BF16)
    z = jnp.dot(first, basis[...], preferred_element_type=F32)
    for q in range(SPAN):
        env = geo[r, 10, pl.ds(n0 + q, 8, stride=0), :]
        slope = geo[r, 11, pl.ds(n0 + q, 8, stride=0), :]
        env, slope = (jnp.concatenate([v] * 8, axis=0) for v in (env, slope))
        zq = z[:, 128 * q : 128 * q + 128]
        zd = z[:, 128 * (SPAN + q) : 128 * (SPAN + q) + 128]
        sig = sigmoid(zq)
        act = zq * sig
        h = act * env
        hd = (sig + act * (1.0 - sig)) * zd * env + act * slope
        for v, at in ((h, q), (hd, SPAN + q)):
            hi, lo = split(v)
            lanes = slice(128 * at, 128 * at + 128)
            hid[0:64, lanes] = hi
            hid[64:128, lanes] = lo
            hid[128:192, lanes] = hi
    w = jnp.dot(second, hid[...], preferred_element_type=F32)
    for q in range(SPAN):
        wgt[r, n0 + q, 0] = w[:, 128 * q : 128 * q + 128]
        wgt[r, n0 + q, 1] = w[:, 128 * (SPAN + q) : 128 * (SPAN + q) + 128]


STAGES = ((0, 2), (2, 6), (6, 9))


def gather(r, stage, step, place, fx, got):
    n0 = step * 2
    first, last = STAGES[stage]
    ids = lax.broadcasted_iota(jnp.int32, (128, 128), 0).astype(F32).astype(BF16)
    halves = []
    for q in range(2):
        at = place[r, pl.ds(n0 + q, 16, stride=0), :]
        j = (at & 127).astype(F32)
        kk = at >> 7
        pieces = []
        for b in range(first, last):
            val = jnp.where(kk == b, j, -1.0).astype(BF16)
            val = jnp.concatenate([val] * 8, axis=0)
            pieces.append(jnp.where(val == ids, jnp.ones((), BF16), jnp.zeros((), BF16)))
        halves.append(jnp.concatenate(pieces, axis=0))
    hot = jnp.concatenate(halves, axis=1)
    rows = [fx[block_at(r, b)] for b in range(first, last)]
    out = jnp.dot(jnp.concatenate(rows, axis=1), hot, preferred_element_type=F32)
    for q in range(2):
        part = out[:, 128 * q : 128 * q + 128]
        got[r, n0 + q] = part if stage == 0 else got[r, n0 + q] + part


def hot_rows(r, place, hot_t):
    j = (place[r] & 127).astype(F32)
    cols = jnp.concatenate([j, jnp.zeros((104, 128), F32)], axis=0).T
    ids = lax.broadcasted_iota(jnp.int32, (128, 128), 1).astype(F32)
    for n in range(24):
        same = jnp.broadcast_to(cols[:, n : n + 1], (128, 128)) == ids
        hot_t[r, 128 * n : 128 * n + 128, :] = jnp.where(same, 1.0, 0.0).astype(BF16)


def row8(ref, r, q, n, times=1):
    v = ref[r, q, pl.ds(n, 8, stride=0), :]
    return v if times == 1 else jnp.concatenate([v] * times, axis=0)


TILE = 16


def aggregate(step, geo, wgt, got, agg):
    per = 64 // TILE
    r = step // per
    c0 = pl.multiple_of((step % per) * TILE, TILE)

    def body(n, acc):
        acc = list(acc)
        y = [None] + [row8(geo, r, q, n, TILE // 8) for q in range(8)]
        x = [got[r, n, pl.ds(m * 64 + c0, TILE), :] for m in range(9)]
        w = [wgt[r, n, 0, pl.ds(p * 64 + c0, TILE), :] for p in range(3)]
        p0 = w[0] * x[0]
        v = x[1] * y[1] + x[2] * y[2] + x[3] * y[3]
        acc[0] += p0 + w[1] * x[0] + w[2] * v
        for m in range(1, 9):
            acc[m] += p0 * y[m] + w[1] * x[m]
        return tuple(acc)

    acc = lax.fori_loop(0, 24, body, (jnp.zeros((TILE, 128), F32),) * 9, unroll=8)
    for m in range(9):
        agg[r, m, pl.ds(c0, TILE), :] = acc[m]


def readout(agg, read3, read_t3, w_out, energies):
    inv = []
    for r in range(2):
        a = [agg[r, m] for m in range(9)]
        sq = [v * v for v in a]
        inv.append(
            jnp.concatenate(
                [sq[0], sq[1] + sq[2] + sq[3], sq[4] + sq[5] + sq[6] + sq[7] + sq[8]], axis=0
            )
        )
    s = jnp.concatenate(inv, axis=1)
    hi, lo = split(s)
    z = jnp.dot(read3, jnp.concatenate([hi, lo, hi], axis=0), preferred_element_type=F32)
    sig = sigmoid(z)
    act = z * sig
    energy = jnp.sum(w_out * act, axis=0, keepdims=True)
    energies[0] = energy[:, :128]
    energies[1] = energy[:, 128:]
    gz = w_out * (sig + act * (1.0 - sig))
    hi, lo = split(gz)
    gs = jnp.dot(read_t3, jnp.concatenate([hi, lo, hi], axis=0), preferred_element_type=F32)
    gs = gs + gs
    for r in range(2):
        g = gs[:, 128 * r : 128 * r + 128]
        for m in range(9):
            part = 0 if m == 0 else 1 if m < 4 else 2
            agg[r, m] = agg[r, m] * g[64 * part : 64 * part + 64]


def backward(step, geo, wgt, got, agg, slopes):
    r = step // 24
    n = step % 24
    y = [None] + [row8(geo, r, q, n) for q in range(8)]
    acc = [jnp.zeros((8, 128), F32)] * 9
    for c in range(8):
        x = [got[r, n, m * 64 + 8 * c : m * 64 + 8 * c + 8, :] for m in range(9)]
        g = [agg[r, m, 8 * c : 8 * c + 8, :] for m in range(9)]
        w0, _, w2 = [wgt[r, n, 0, p * 64 + 8 * c : p * 64 + 8 * c + 8, :] for p in range(3)]
        d0, d1, d2 = [wgt[r, n, 1, p * 64 + 8 * c : p * 64 + 8 * c + 8, :] for p in range(3)]
        gx = g[0] * x[0]
        gy = g[0]
        for m in range(1, 9):
            gx += g[m] * x[m]
            gy += g[m] * y[m]
        v = x[1] * y[1] + x[2] * y[2] + x[3] * y[3]
        acc[0] += d1 * gx + d0 * (gy * x[0]) + d2 * (g[0] * v)
        p0 = w0 * x[0]
        p2 = w2 * g[0]
        for m in range(1, 9):
            acc[m] += p0 * g[m] + p2 * x[m] if m < 4 else p0 * g[m]
    for q in range(9):
        slopes[r, q, pl.ds(n, 1), :] = jnp.sum(acc[q], axis=0, keepdims=True)


def edge_forces(r, geo, unit, slopes, edge):
    r3, r5, r15 = math.sqrt(3.0), math.sqrt(5.0), math.sqrt(15.0)
    ux, uy, uz = (unit[r, q] for q in range(3))
    rinv = geo[r, 9]
    gd, g1, g2, g3, g4, g5, g6, g7, g8 = (slopes[r, q] for q in range(9))
    gx = r3 * g1 + r15 * (uy * g4 + uz * g7 + ux * g8)
    gy = r3 * g2 + r15 * (ux * g4 + uz * g5 - uy * g8)
    gz = r3 * g3 + r15 * (uy * g5 + ux * g7) + (3.0 * r5) * uz * g6
    along = gd - (gx * ux + gy * uy + gz * uz) * rinv
    out = []
    for q, (g, u) in enumerate(((gx, ux), (gy, uy), (gz, uz))):
        f = g * rinv + along * u
        edge[q] = f
        out.append(jnp.sum(f, axis=0, keepdims=True))
    return out


def scatter(r, place, edge, lhs, hot_t, centre, forces):
    pick = lax.broadcasted_iota(jnp.int32, (8, 128), 0)

    def body(n, carry):
        kk = place[r, pl.ds(n, 8, stride=0), :] >> 7
        value = jnp.zeros((8, 128), F32)
        for q in range(3):
            f = edge[q, pl.ds(n, 8, stride=0), :]
            hi = f.astype(BF16).astype(F32)
            value = jnp.where(pick == q, hi, jnp.where(pick == q + 3, f - hi, value))
        rows = [jnp.where(kk == b, value, 0.0) for b in range(9)] + [jnp.zeros((8, 128), F32)]
        lanes = pl.ds(pl.multiple_of(n * 128, 128), 128)
        lhs[:, lanes] = jnp.concatenate(rows, axis=0).astype(BF16)
        return carry

    lax.fori_loop(0, 24, body, 0, unroll=4)
    out = jnp.dot(lhs[...], hot_t[r], preferred_element_type=F32)
    for b in range(9):
        row, role = block_at(r, b)
        for q in range(3):
            v = -(out[8 * b + q : 8 * b + q + 1] + out[8 * b + q + 3 : 8 * b + q + 4])
            if row == r + 1 and role == 0:
                v += centre[q]
            forces[role, row, q] += v


def stack(w, axis):
    hi, lo = split(w)
    return jnp.concatenate([hi, hi, lo], axis=axis)


POS = 0
VEL = 8
OWN = 9
CHIP = 13
OFF = 14
CORNER = 15
FAR = 17
NEAR_CHIP = 21
FAR_CHIP = 22
FAR_CORNER = 23
TAIL = 25
COPIES = 30
AROUND = ((-1, -1), (-1, 0), (-1, 1), (0, -1), (0, 1), (1, -1), (1, 0), (1, 1))
BACK = ((0, 1), (0, -1), (-1, 1), (-1, 0), (-1, -1))


def step_kernel(
    positions_in, velocities_in, features, codes_in, counts_in, w_first_in, w_second_in, w_read_in,
    w_out_in, fresh_pos_in, fresh_vel_in, energies, new_pos, new_vel,
    positions, velocities, codes, counts, w_first, w_second, w_read, w_out, fresh_pos, fresh_vel,
    pos, vel_in, fx, place, geo, unit, basis, hid, wgt, got, agg, slopes, edge, lhs, hot_t,
    forces, tail, first, second, read3, read_t3, out_col, own_sem, load_sem, send_sem, recv_sem,
):
    s = lax.axis_index("shock")
    t = lax.axis_index("trans")
    ns = lax.axis_size("shock")
    nt = lax.axis_size("trans")
    core = lax.rem(s, 2)
    way = 1 - 2 * lax.rem(t, 2)
    out_way = 2 * core - 1

    def at(ds, dt):
        return (lax.rem(s + ds + ns, ns), lax.rem(t + dt + nt, nt))

    def copy(k, src, dst, to):
        return pltpu.make_async_remote_copy(
            src_ref=src,
            dst_ref=dst,
            send_sem=send_sem.at[k],
            recv_sem=recv_sem.at[k],
            device_id=to,
            device_id_type=pl.DeviceIdType.MESH,
        )

    barrier = pltpu.get_barrier_semaphore()
    for ds, dt in AROUND + ((0, 2), (0, -2)):
        pl.semaphore_signal(
            barrier, inc=1, device_id=at(ds, dt), device_id_type=pl.DeviceIdType.MESH
        )
    own = pltpu.make_async_copy(features.at[:, 0], fx.at[pl.ds(1, 2), 0], own_sem)
    loads = [
        pltpu.make_async_copy(src, dst, load_sem.at[i])
        for i, (src, dst) in enumerate(
            (
                (codes_in, codes),
                (positions_in, positions),
                (counts_in, counts),
                (w_first_in, w_first),
                (w_second_in, w_second),
                (w_read_in, w_read),
                (w_out_in, w_out),
                (velocities_in, velocities),
                (fresh_pos_in, fresh_pos),
                (fresh_vel_in, fresh_vel),
                (positions_in, pos.at[pl.ds(1, 2), 0]),
            )
        )
    ]
    own.start()
    for load in loads:
        load.start()
    pl.semaphore_wait(barrier, 10)

    flights = {}

    def role(dt):
        return 0 if dt == 0 else (3 - dt * way) // 2

    for i, (ds, dt) in enumerate(AROUND):
        if ds == 0:
            src, dst = positions_in, pos.at[pl.ds(1, 2), role(dt)]
        elif ds == 1:
            src, dst = positions_in.at[1], pos.at[0, role(dt)]
        else:
            src, dst = positions_in.at[0], pos.at[3, role(dt)]
        flights[POS + i] = copy(POS + i, src, dst, at(ds, dt))
    flights[VEL] = copy(VEL, velocities_in.at[0], vel_in, at(-1, 0))
    chip_row, chip_ghost = 1 - core, 3 * core
    off_row, off_ghost = core, 3 * (1 - core)
    order = (chip_row, off_row)
    my_off_ghost = 3 * core
    for i in range(4):
        row, half = 1 + order[i // 2], pl.ds(288 * (i % 2), 288)
        flights[OWN + i] = copy(
            OWN + i, features.at[row - 1, 0, half], fx.at[row, 1, half], at(0, way)
        )
        flights[FAR + i] = copy(
            FAR + i, fx.at[row, 1, half], fx.at[row, 2, half], at(0, 2 * way)
        )
    flights[CHIP] = copy(CHIP, features.at[chip_row, 0], fx.at[chip_ghost, 0], at(-out_way, 0))
    flights[OFF] = copy(OFF, features.at[off_row, 0], fx.at[off_ghost, 0], at(out_way, 0))
    for i in range(2):
        half = pl.ds(288 * i, 288)
        flights[CORNER + i] = copy(
            CORNER + i, features.at[off_row, 0, half], fx.at[off_ghost, 1, half], at(out_way, way)
        )
        flights[FAR_CORNER + i] = copy(
            FAR_CORNER + i, fx.at[my_off_ghost, 1, half], fx.at[my_off_ghost, 2, half], at(0, 2 * way)
        )
    for k in [OWN, *range(POS, POS + 8), *range(OWN + 1, OWN + 4), CHIP, CORNER, CORNER + 1, OFF, VEL]:
        flights[k].start()
    flights[NEAR_CHIP] = copy(
        NEAR_CHIP, fx.at[1 + chip_row, 1], fx.at[chip_ghost, 1], at(-out_way, 0)
    )
    flights[FAR_CHIP] = copy(
        FAR_CHIP, fx.at[1 + chip_row, 2], fx.at[chip_ghost, 2], at(-out_way, 0)
    )

    def gather_stage(r, stage, first_step=0, last_step=12):
        def gather_step(step, carry):
            gather(r, stage, step, place, fx, got)
            return carry

        lax.fori_loop(first_step, last_step, gather_step, 0, unroll=last_step - first_step)

    def pass_on(k, to):
        flights[k].wait_recv()
        flights[to].start()

    loads[0].wait()
    for r in range(2):
        places(r, way, codes, place)
    own.wait()
    gather_stage(0, 0)
    gather_stage(1, 0)
    pass_on(OWN, FAR)

    for load in loads[1:]:
        load.wait()
    first[...] = jnp.concatenate([stack(w_first[...].T, 1), jnp.zeros((64, 8), BF16)], axis=1)
    second[...] = stack(w_second[...].T, 1)
    read3[...] = stack(w_read[...].T, 1)
    read_t3[...] = stack(w_read[...], 1)
    col = jnp.broadcast_to(w_out[...], (128, 128)).T
    out_col[...] = jnp.concatenate([col, col], axis=1)
    hot_rows(0, place, hot_t)
    pass_on(OWN + 1, FAR + 1)
    flights[NEAR_CHIP].start()
    hot_rows(1, place, hot_t)

    for k in range(POS, POS + 8):
        flights[k].wait_recv()

    @pl.when(s == 0)
    def _():
        pos[0] = jnp.zeros((3, 3, 1, 128), F32)

    @pl.when(s == ns - 1)
    def _():
        pos[3] = jnp.zeros((3, 3, 1, 128), F32)

    for r in range(2):
        geometry(r, pos, codes, place, counts, geo, unit)

    def radial_step(step, carry):
        radial(step, geo, first[...], second[...], basis, hid, wgt)
        return carry

    pass_on(OWN + 2, FAR + 2)
    lax.fori_loop(0, 24 // SPAN, radial_step, 0)
    pass_on(OWN + 3, FAR + 3)
    lax.fori_loop(24 // SPAN, 48 // SPAN, radial_step, 0)
    flights[FAR].wait_recv()
    flights[FAR + 1].wait_recv()
    flights[FAR_CHIP].start()
    pass_on(CORNER, FAR_CORNER)
    flights[CHIP].wait_recv()
    flights[NEAR_CHIP].wait_recv()
    gather_stage(1 - core, 1, 0, 6)
    pass_on(CORNER + 1, FAR_CORNER + 1)
    gather_stage(1 - core, 1, 6, 12)
    flights[OFF].wait_recv()
    for i in range(2):
        flights[FAR_CORNER + i].wait_send()
    blank = jnp.zeros((576, 128), BF16)

    def close(role):
        @pl.when(s == 0)
        def _():
            fx[0, role] = blank

        @pl.when(s == ns - 1)
        def _():
            fx[3, role] = blank

    close(0)
    close(1)
    gather_stage(core, 1)
    for k in (FAR + 2, FAR + 3, FAR_CHIP):
        flights[k].wait_recv()
    gather_stage(1 - core, 2)

    def aggregate_row(r):
        def aggregate_step(step, carry):
            aggregate(r * (64 // TILE) + step, geo, wgt, got, agg)
            return carry

        lax.fori_loop(0, 64 // TILE, aggregate_step, 0)

    aggregate_row(1 - core)
    for i in range(2):
        flights[FAR_CORNER + i].wait_recv()
    close(2)
    gather_stage(core, 2)
    aggregate_row(core)
    readout(agg, read3[...], read_t3[...], out_col[...], energies)

    def backward_step(step, carry):
        backward(step, geo, wgt, got, agg, slopes)
        return carry

    lax.fori_loop(0, 48, backward_step, 0, unroll=4)
    forces[...] = jnp.zeros_like(forces)
    for r in range(2):
        centre = edge_forces(r, geo, unit, slopes, edge)
        scatter(r, place, edge, lhs, hot_t, centre, forces)

    for i, (ds, dt) in enumerate(BACK):
        src = forces.at[role(dt), pl.ds(2 if ds == 0 else 0, 2)]
        flights[TAIL + i] = copy(TAIL + i, src, tail.at[i], at(ds, dt))
        flights[TAIL + i].start()
    for k in list(range(FAR_CORNER)):
        flights[k].wait_send()
    flights[VEL].wait_recv()
    for i in range(5):
        flights[TAIL + i].wait_recv()
    front = s == ns - 1
    above = tail[2] + tail[3] + tail[4]
    force = forces[0, 2:4] + tail[0] + tail[1] + jnp.where(front, 0.0, above)
    vel = velocities[1] + KICK_FACTOR * force[0]
    new_vel[0] = vel
    new_pos[0] = positions[1] + MOVE_FACTOR * vel
    vel = vel_in[...] + KICK_FACTOR * force[1]
    new_vel[1] = jnp.where(front, fresh_vel[...], vel)
    new_pos[1] = jnp.where(front, fresh_pos[...], pos[3, 0] + MOVE_FACTOR * vel)
    for i in range(5):
        flights[TAIL + i].wait_send()


def local(
    positions, velocities, features, neighbours, counts, w_first, w_second, w_read, w_out,
    fresh_positions, fresh_velocities,
):
    vmem = pl.BlockSpec(memory_space=pltpu.VMEM)
    whole = pl.BlockSpec(memory_space=pl.ANY)
    energies, new_pos, new_vel = pl.pallas_call(
        step_kernel,
        out_shape=(
            pltpu.VMEM((2, 1, 128), F32),
            pltpu.VMEM((2, 3, 1, 128), F32),
            pltpu.VMEM((2, 3, 1, 128), F32),
        ),
        in_specs=[whole] * 11,
        out_specs=(vmem, vmem, vmem),
        scratch_shapes=[
            pltpu.VMEM((2, 3, 1, 128), F32),
            pltpu.VMEM((2, 3, 1, 128), F32),
            pltpu.VMEM((2, 1, 24, 128), jnp.int32),
            pltpu.VMEM((2, 1, 128), jnp.int32),
            pltpu.VMEM((8, 64), F32),
            pltpu.VMEM((64, 192), F32),
            pltpu.VMEM((192, 128), F32),
            pltpu.VMEM((1, 128), F32),
            pltpu.VMEM((3, 1, 128), F32),
            pltpu.VMEM((3, 1, 128), F32),
            pltpu.VMEM((4, 3, 3, 1, 128), F32),
            pltpu.VMEM((3, 1, 128), F32),
            pltpu.VMEM((4, 3, 576, 128), BF16),
            pltpu.VMEM((2, 24, 128), jnp.int32),
            pltpu.VMEM((2, GEO, 24, 128), F32),
            pltpu.VMEM((2, 3, 24, 128), F32),
            pltpu.VMEM((32, 256 * SPAN), BF16),
            pltpu.VMEM((192, 256 * SPAN), BF16),
            pltpu.VMEM((2, 24, 2, 192, 128), F32),
            pltpu.VMEM((2, 24, 576, 128), F32),
            pltpu.VMEM((2, 9, 64, 128), F32),
            pltpu.VMEM((2, 9, 24, 128), F32),
            pltpu.VMEM((3, 24, 128), F32),
            pltpu.VMEM((80, 3072), BF16),
            pltpu.VMEM((2, 3072, 128), BF16),
            pltpu.VMEM((3, 4, 3, 1, 128), F32),
            pltpu.VMEM((5, 2, 3, 1, 128), F32),
            pltpu.VMEM((64, 32), BF16),
            pltpu.VMEM((192, 192), BF16),
            pltpu.VMEM((128, 576), BF16),
            pltpu.VMEM((192, 384), BF16),
            pltpu.VMEM((128, 256), F32),
            pltpu.SemaphoreType.DMA,
            pltpu.SemaphoreType.DMA((11,)),
            pltpu.SemaphoreType.DMA((COPIES,)),
            pltpu.SemaphoreType.DMA((COPIES,)),
        ],
        compiler_params=pltpu.CompilerParams(
            vmem_limit_bytes=56 << 20, collective_id=0, has_side_effects=True
        ),
        name="step",
    )(
        positions.transpose(0, 2, 1, 3), velocities.transpose(0, 2, 1, 3), features, neighbours,
        counts, w_first.T, w_second.T, w_read.T, w_out[None],
        fresh_positions.transpose(1, 0, 2), fresh_velocities.transpose(1, 0, 2),
    )
    return energies, new_pos.transpose(0, 2, 1, 3), new_vel.transpose(0, 2, 1, 3)


def solution(mesh):
    spec = P("shock", "trans", None, None)
    return jax.shard_map(
        local,
        mesh=mesh,
        in_specs=(
            spec, spec, spec, spec, P("shock", "trans", None), P(), P(), P(), P(),
            P("trans", None, None), P("trans", None, None),
        ),
        out_specs=(P("shock", "trans", None), spec, spec),
        check_vma=False,
    )
```
